256 devices in a mesh: tm: 32 (over y, z_lo, core), space: 8 (over z_hi, x).
Axes of the slice: x: 4, y: 4, z: 8 (z_hi: 2, z_lo: 4; z = z_hi * 4 + z_lo), core: 2. Of those that a mesh axis runs over, the one named last changes fastest.
Arguments:
- queries: bfloat16 [32768, 4096], P(('tm', 'space')), may hold values from -14 to 14
- keys: bfloat16 [32768, 2048], P(('tm', 'space')), may hold values from -6 to 6
- values: bfloat16 [32768, 2048], P(('tm', 'space')), may hold values from -6 to 6
- output_gradient: bfloat16 [32768, 4096], P(('tm', 'space')), may hold values from -6 to 6
- tiles: int32 [256, 6], P('tm'), may hold values from 0 to 23, as said below
- kinds: int32 [256, 6], P('tm'), may hold values from 0 to 2, as said below
Outputs:
- grad_queries: bfloat16 [32768, 4096], P(('tm', 'space'))
- grad_keys: bfloat16 [32768, 2048], P(('tm', 'space'))
- grad_values: bfloat16 [32768, 2048], P(('tm', 'space'))
The draws below stay inside these ranges and needn't reach their ends.
Inputs may be any that keep to these rules, and one draw needn't show every extreme that they name: Row b lists the key tiles of query block b, which lies in window w = b // 8 at block b % 8 of it. A value v names kv block v % 8 of window w - v // 8; windows below 0 are never named, nor, where v // 8 = 0, blocks at or after b % 8 except in slot 0. Slot 0 holds b % 8; slots 1 to u hold distinct other values, u from 0 to 5, ragged over the blocks; the remaining slots hold 0. Every draw has rows with u = 5 and names the largest value. `kinds`: kind 0: every key of the tile is visible; kind 1: a key is visible when its position in its tile is at most the query's position in its block; kind 2: the slot is unused. Slot 0 has kind 1, used slots kind 0 or 1, unused slots kind 2.
All inputs are finite; a program needn't handle non-finite values.
Results may differ from the reference program's by a relative error of at most 0.015.
Values may be sent and summed in bfloat16 or wider, within the bound.
A program may use at most 128 MiB of HBM per device.

```python
import jax
import jax.numpy as jnp
from jax import lax

QUERY_HEAD_COUNT = 32
KEY_VALUE_HEADS = 16
HEAD_SIZE = 128
BLOCK_TOKENS = 128
MAXT = 6
REACH = 2
KBW = 8
SEQUENCE_TOKENS = 32768
QUERY_BLOCK_COUNT = 256


def draw_keys(key, part):
    unsigned_tiles = jnp.clip(jax.random.normal(jax.random.fold_in(key, 1), (SEQUENCE_TOKENS, KEY_VALUE_HEADS * HEAD_SIZE), jnp.float32), -6.0, 6.0)
    return unsigned_tiles.astype(jnp.bfloat16)


def draw_queries(key, part):
    unsigned_tiles = jnp.clip(jax.random.normal(jax.random.fold_in(key, 4), (SEQUENCE_TOKENS, QUERY_HEAD_COUNT * HEAD_SIZE), jnp.float32), -6.0, 6.0)
    return unsigned_tiles.astype(jnp.bfloat16)


def tile_plan(key):
    block = jnp.arange(QUERY_BLOCK_COUNT, dtype=jnp.int32)
    window = block // KBW
    own_block = block % KBW
    cells = (REACH + 1) * KBW
    candidate = jnp.arange(cells, dtype=jnp.int32)
    distance = candidate // KBW
    column = candidate % KBW
    valid = (distance[None, :] <= window[:, None]) & ((distance[None, :] > 0) | (column[None, :] < own_block[:, None]))
    last_row = (own_block == KBW - 1) & (window >= REACH)
    forced = last_row[:, None] & (candidate[None, :] == cells - 1)
    noise = jax.random.randint(jax.random.fold_in(key, 201), (QUERY_BLOCK_COUNT, cells), 0, 1 << 20, dtype=jnp.int32)
    ranking = noise * cells + candidate[None, :]
    ranking = jnp.where(valid, ranking, ranking + (1 << 30))
    ranking = jnp.where(forced, -1, ranking)
    ordered = jnp.argsort(ranking, axis=1, stable=True)[:, :MAXT - 1].astype(jnp.int32)
    valid_count = jnp.sum(valid.astype(jnp.int32), axis=1)
    wanted = jax.random.randint(jax.random.fold_in(key, 202), (QUERY_BLOCK_COUNT,), 0, MAXT, dtype=jnp.int32)
    wanted = jnp.where(last_row, MAXT - 1, wanted)
    used_count = jnp.minimum(wanted, valid_count)
    slot = jnp.arange(1, MAXT, dtype=jnp.int32)
    active = slot[None, :] <= used_count[:, None]
    extra_tiles = jnp.where(active, ordered, 0)
    extra_kinds = jax.random.randint(jax.random.fold_in(key, 203), (QUERY_BLOCK_COUNT, MAXT - 1), 0, 2, dtype=jnp.int32)
    extra_kinds = jnp.where(last_row[:, None] & (slot[None, :] == 1), 0, extra_kinds)
    extra_kinds = jnp.where(active, extra_kinds, 2)
    tile_table = jnp.concatenate([own_block[:, None], extra_tiles], axis=1).astype(jnp.int32)
    kind_table = jnp.concatenate([jnp.ones((QUERY_BLOCK_COUNT, 1), jnp.int32), extra_kinds], axis=1).astype(jnp.int32)
    return (tile_table, kind_table)


def draw_tiles(key, part):
    return tile_plan(key)[0]


def draw_kinds(key, part):
    return tile_plan(key)[1]


def block_levels(own_key, dims, shards, low, top_value):
    gain = 1.0
    for dim, shards_of in shards:
        draws = jax.random.uniform(jax.random.fold_in(jax.random.fold_in(own_key, 6), dim), (shards_of,), jnp.float32, low / len(shards), top_value / len(shards))
        gain = gain * jnp.repeat(jnp.exp(draws), dims[dim] // shards_of).reshape((-1,) + (1,) * (len(dims) - 1 - dim))
    return gain


def scatter_about(stream_key, shape, deviation, reach, split=(), held_as=jnp.bfloat16):
    values = jax.random.normal(stream_key, shape, jnp.float32) * deviation
    if len(split) > 0:
        values = block_levels(stream_key, shape, split, -0.22, 0.18) * values
    return jnp.clip(values, min=-reach, max=reach).astype(held_as)


def setup_inputs(seed: int = 0) -> dict:
    seeds = jax.random.split(jax.random.key(seed), 7)
    return {
        "queries": draw_queries(jax.random.fold_in(seeds[6], 71), 0),
        "keys": draw_keys(jax.random.fold_in(seeds[6], 71), 0),
        "values": scatter_about(seeds[2], (SEQUENCE_TOKENS, KEY_VALUE_HEADS * HEAD_SIZE), 1.0, 6.0, ((0, 256),)),
        "output_gradient": scatter_about(seeds[3], (SEQUENCE_TOKENS, QUERY_HEAD_COUNT * HEAD_SIZE), 1.0, 6.0, ((0, 256),)),
        "tiles": draw_tiles(jax.random.fold_in(seeds[6], 71), 0),
        "kinds": draw_kinds(jax.random.fold_in(seeds[6], 71), 0),
    }


def block_grads(query_rows, grad_rows, key_tiles, value_tiles, tile_kinds):
    blocks, length, kv_count, head_dim = key_tiles.shape
    score_scale = 1.0 / (head_dim ** 0.5)
    key_flat = key_tiles.reshape(blocks * length, kv_count, head_dim)
    value_flat = value_tiles.reshape(blocks * length, kv_count, head_dim)
    highest = lax.Precision.HIGHEST
    scores = jnp.einsum("qkgd,tkd->kgqt", query_rows, key_flat, precision=highest) * score_scale
    query_pos = jnp.arange(length)
    column_kind = jnp.repeat(tile_kinds, length)
    column_pos = jnp.tile(jnp.arange(length), blocks)
    visible = (column_kind == 0)[None, :] | ((column_kind == 1)[None, :] & (column_pos[None, :] <= query_pos[:, None]))
    masked = jnp.where(visible, scores, -jnp.inf)
    row_max = jnp.max(masked, axis=-1, keepdims=True)
    weights = jnp.where(visible, jnp.exp(masked - row_max), 0.0)
    probabilities = weights / jnp.sum(weights, axis=-1, keepdims=True)
    probs_low = probabilities.astype(jnp.bfloat16).astype(jnp.float32)
    outputs = jnp.einsum("kgqt,tkd->qkgd", probs_low, value_flat, precision=highest)
    row_delta = jnp.einsum("qkgd,qkgd->kgq", grad_rows, outputs, precision=highest)
    grad_probs = jnp.einsum("qkgd,tkd->kgqt", grad_rows, value_flat, precision=highest)
    grad_scores = (score_scale * probabilities * (grad_probs - row_delta[..., None])).astype(jnp.bfloat16).astype(jnp.float32)
    grad_query = jnp.einsum("kgqt,tkd->qkgd", grad_scores, key_flat, precision=highest)
    grad_key = jnp.einsum("kgqt,qkgd->tkd", grad_scores, query_rows, precision=highest)
    grad_value = jnp.einsum("kgqt,qkgd->tkd", probs_low, grad_rows, precision=highest)
    return (grad_query.astype(jnp.bfloat16),
            grad_key.reshape(blocks, length, kv_count, head_dim),
            grad_value.reshape(blocks, length, kv_count, head_dim))


def reference(queries, keys, values, output_gradient, tiles, kinds):
    head_groups = QUERY_HEAD_COUNT // KEY_VALUE_HEADS
    key_block_rows = keys.reshape(QUERY_BLOCK_COUNT, BLOCK_TOKENS, KEY_VALUE_HEADS, HEAD_SIZE)
    value_block_rows = values.reshape(QUERY_BLOCK_COUNT, BLOCK_TOKENS, KEY_VALUE_HEADS, HEAD_SIZE)
    query_block_rows = queries.reshape(QUERY_BLOCK_COUNT, BLOCK_TOKENS, KEY_VALUE_HEADS, head_groups, HEAD_SIZE)
    block_gradients = output_gradient.reshape(QUERY_BLOCK_COUNT, BLOCK_TOKENS, KEY_VALUE_HEADS, head_groups, HEAD_SIZE)

    def advance(totals, block_index):
        summed_key_grad, summed_value_grad = totals
        window = block_index // KBW
        tile_row = tiles[block_index]
        source = ((window - tile_row // KBW) * KBW + tile_row % KBW).astype(jnp.int32)
        grad_query, grad_key, grad_value = block_grads(
            query_block_rows[block_index].astype(jnp.float32),
            block_gradients[block_index].astype(jnp.float32),
            key_block_rows[source].astype(jnp.float32),
            value_block_rows[source].astype(jnp.float32),
            kinds[block_index])
        return (summed_key_grad.at[source].add(grad_key), summed_value_grad.at[source].add(grad_value)), grad_query

    blank_total_sum = jnp.zeros((QUERY_BLOCK_COUNT, BLOCK_TOKENS, KEY_VALUE_HEADS, HEAD_SIZE), jnp.float32)
    (summed_key_grad, summed_value_grad), grad_queries = lax.scan(advance, (blank_total_sum, blank_total_sum), jnp.arange(QUERY_BLOCK_COUNT, dtype=jnp.int32))
    return (grad_queries.reshape(SEQUENCE_TOKENS, QUERY_HEAD_COUNT * HEAD_SIZE),
            summed_key_grad.reshape(SEQUENCE_TOKENS, KEY_VALUE_HEADS * HEAD_SIZE).astype(jnp.bfloat16),
            summed_value_grad.reshape(SEQUENCE_TOKENS, KEY_VALUE_HEADS * HEAD_SIZE).astype(jnp.bfloat16))
```

```python
import functools

import jax
import jax.numpy as jnp
from jax import lax
from jax.experimental import pallas as pl
from jax.experimental.pallas import tpu as pltpu
from jax.sharding import PartitionSpec as P

HEAD = 128
BLOCK = 128
MAXT = 6
HEADS = 4
UNITS = 2 * HEADS
TILES = 24
PLUS = (1, 4, 6)
MINUS = (0, 2, 3, 5, 7)
X_ORDER = (0, 1, 2, 4, 3, 6, 5, 7)
MESH = pl.DeviceIdType.MESH
LOG2E = 1.4426950408889634


def place():
    tm = lax.axis_index("tm")
    space = lax.axis_index("space")
    core = lax.rem(tm, 2)
    z_lo = lax.rem(lax.div(tm, 2), 4)
    x = lax.rem(space, 4)
    z_hi = lax.div(space, 4)
    return tm, core, x, z_hi, z_hi * 4 + z_lo


def ring_peers():
    tm, core, x, z_hi, z = place()

    def at(tm_step, z_step):
        there = lax.rem(z + z_step, 8)
        return {"tm": lax.rem(tm + tm_step, 32), "space": lax.div(there, 4) * 4 + x}

    right, left, far_right, far_left = at(2, 1), at(30, 7), at(2, 5), at(30, 3)
    partner = {"tm": tm + 1 - 2 * core, "space": z_hi * 4 + x}
    along_x = [{"tm": tm, "space": z_hi * 4 + lax.rem(x + d, 4)} for d in (1, 2, 3)]
    return right, left, far_right, far_left, partner, along_x


def meet(peers):
    barrier = pltpu.get_barrier_semaphore()
    for peer in peers:
        pl.semaphore_signal(barrier, inc=1, device_id=peer, device_id_type=MESH)
    pl.semaphore_wait(barrier, len(peers))


def send(src, dst, sems, index, device):
    send_sem, recv_sem = sems
    copy = pltpu.make_async_remote_copy(
        src_ref=src,
        dst_ref=dst,
        send_sem=send_sem.at[index],
        recv_sem=recv_sem.at[index],
        device_id=device,
        device_id_type=MESH,
    )
    copy.start()
    return copy


def columns(start, width):
    return pl.ds(pl.multiple_of(start, width), width)


def gather_kernel(
    q_ref, k_ref, v_ref, g_ref, kv_ref, qh_ref, gh_ref,
    xs, xr, qs, qr, s1, r1, s2, r2, s3, r3, sp, rp, local,
):
    tm, core, x, z_hi, z = place()
    right, left, far_right, far_left, partner, along_x = ring_peers()
    from_left = lax.div(lax.rem(z + 7, 8), 4)
    from_far = 1 - from_left
    opposite = 1 - z_hi
    meet([right, left, far_right, far_left, partner] + along_x)

    def quad(window, half):
        return pl.ds(window * 8 + half * 4, 4)

    def source(unit, to_x):
        ref = v_ref if unit % 2 else k_ref
        return ref.at[:, columns((to_x * HEADS + unit // 2) * HEAD, HEAD)]

    waits = []
    x_copies = {}
    own_copies = {}
    for unit in X_ORDER:
        x_copies[unit] = [
            send(source(unit, lax.rem(x + d, 4)), kv_ref.at[unit, z_hi * 4 + x],
                 (xs, xr), unit * 3 + d - 1, along_x[d - 1])
            for d in (1, 2, 3)
        ]
        own = pltpu.make_async_copy(source(unit, x), kv_ref.at[unit, z_hi * 4 + x], local.at[unit])
        own.start()
        own_copies[unit] = own
        waits += x_copies[unit]
    q_copies = []
    for i, (ref, to) in enumerate(((q_ref, qh_ref), (g_ref, gh_ref))):
        for d in (1, 2, 3):
            q_copies.append(
                send(ref.at[:, columns(lax.rem(x + d, 4) * 1024, 1024)], to.at[x],
                     (qs, qr), i * 3 + d - 1, along_x[d - 1])
            )
        own = pltpu.make_async_copy(ref.at[:, columns(x * 1024, 1024)], to.at[x], local.at[UNITS + i])
        own.start()
        own_copies[UNITS + i] = own
    waits += q_copies

    first, second, third = {}, {}, {}

    def to_right(unit):
        piece = kv_ref.at[unit, quad(0, z_hi)]
        first[unit] = send(piece, kv_ref.at[unit, quad(2, z_hi)], (s1, r1), unit, right)

    for unit in X_ORDER:
        own_copies[unit].wait()
        for copy in x_copies[unit]:
            copy.wait_recv()
        if unit in PLUS:
            to_right(unit)
        else:
            piece = kv_ref.at[unit, quad(0, z_hi)]
            second[unit] = send(piece, kv_ref.at[unit, quad(2, z_hi)], (s2, r2), unit, far_right)
    for unit in PLUS:
        first[unit].wait_recv()
        piece = kv_ref.at[unit, quad(2, from_left)]
        second[unit] = send(piece, kv_ref.at[unit, quad(0, from_left)], (s2, r2), unit, far_left)
    for unit in MINUS:
        to_right(unit)

    def to_partner(unit):
        piece = kv_ref.at[unit, pl.ds(core * 16, 8)]
        return send(piece, kv_ref.at[unit, pl.ds(8, 8)], (sp, rp), unit, partner)

    across = []
    for unit in MINUS:
        second[unit].wait_recv()
        piece = kv_ref.at[unit, quad(2, from_far)]
        third[unit] = send(piece, kv_ref.at[unit, quad(0, from_far)], (s3, r3), unit, left)
    for unit in PLUS:
        second[unit].wait_recv()
        piece = kv_ref.at[unit, quad(0, opposite)]
        third[unit] = send(piece, kv_ref.at[unit, quad(2, opposite)], (s3, r3), unit, right)
    for unit in MINUS:
        first[unit].wait_recv()
        third[unit].wait_recv()
        across.append(to_partner(unit))
    for unit in PLUS:
        third[unit].wait_recv()
        across.append(to_partner(unit))
    for copy in q_copies + across:
        copy.wait_recv()
    own_copies[UNITS].wait()
    own_copies[UNITS + 1].wait()
    for table in (first, second, third):
        waits += list(table.values())
    for copy in waits + across:
        copy.wait_send()


def gather(queries, keys, values, grads):
    spec = pl.BlockSpec(memory_space=pltpu.VMEM)
    dma = pltpu.SemaphoreType.DMA
    return pl.pallas_call(
        gather_kernel,
        name="gather_heads",
        out_shape=(
            jax.ShapeDtypeStruct((UNITS, TILES, BLOCK, HEAD), jnp.bfloat16),
            jax.ShapeDtypeStruct((4, BLOCK, 1024), jnp.bfloat16),
            jax.ShapeDtypeStruct((4, BLOCK, 1024), jnp.bfloat16),
        ),
        in_specs=[spec] * 4,
        out_specs=(spec,) * 3,
        scratch_shapes=[dma((24,)), dma((24,)), dma((6,)), dma((6,))]
        + [dma((UNITS,))] * 8
        + [dma((UNITS + 2,))],
        compiler_params=pltpu.CompilerParams(
            collective_id=1, has_side_effects=True, vmem_limit_bytes=24 << 20
        ),
    )(queries, keys, values, grads)


NT = (((1,), (1,)), ((), ()))
NN = (((1,), (0,)), ((), ()))
TN = (((0,), (0,)), ((), ()))


def dot(a, b, dims):
    return lax.dot_general(a, b, dims, preferred_element_type=jnp.float32)


def grads_kernel(tiles_ref, kinds_ref, kv_ref, q_ref, g_ref, dkv_ref, dq_ref, acc):
    scale = 1.0 / HEAD**0.5
    half = lax.div(lax.axis_index("space"), 4)
    acc[...] = jnp.zeros_like(acc)
    row = lax.broadcasted_iota(jnp.int32, (BLOCK, 2 * BLOCK), 0)
    col = lax.broadcasted_iota(jnp.int32, (BLOCK, 2 * BLOCK), 1)
    ahead = row - jnp.where(col >= BLOCK, col - BLOCK, col)
    for b in range(4):
        line = half * 4 + b
        names = [tiles_ref[line, m] for m in range(MAXT)]
        kinds = [kinds_ref[line, m] for m in range(MAXT)]
        k = jnp.concatenate([kv_ref[0, t] for t in names], axis=0)
        v = jnp.concatenate([kv_ref[1, t] for t in names], axis=0)
        q = jnp.concatenate([q_ref[b, :, :HEAD], q_ref[b, :, HEAD:]], axis=0)
        g = jnp.concatenate([g_ref[b, :, :HEAD], g_ref[b, :, HEAD:]], axis=0)
        scores = dot(k, q, NT)
        masked = []
        for m in range(MAXT):
            limit = jnp.where(kinds[m] == 0, BLOCK, jnp.where(kinds[m] == 1, 0, -2 * BLOCK))
            masked.append(
                jnp.where(ahead <= limit, scores[m * BLOCK : (m + 1) * BLOCK], -jnp.inf)
            )
        scores = jnp.concatenate(masked, axis=0)
        top = jnp.max(scores, axis=0, keepdims=True)
        weights = jnp.exp2((scores - top) * (scale * LOG2E))
        probs = weights * (1.0 / jnp.sum(weights, axis=0, keepdims=True))
        low = probs.astype(jnp.bfloat16)
        grad_probs = dot(v, g, NT)
        delta = jnp.sum(low.astype(jnp.float32) * grad_probs, axis=0, keepdims=True)
        grad_scores = (probs * (grad_probs - delta) * scale).astype(jnp.bfloat16)
        grad_values = dot(low, g, NN)
        grad_keys = dot(grad_scores, q, NN)
        grad_q = dot(grad_scores, k, TN).astype(jnp.bfloat16)
        dq_ref[b, :, :HEAD] = grad_q[:BLOCK]
        dq_ref[b, :, HEAD:] = grad_q[BLOCK:]
        for m in range(MAXT):
            rows = slice(m * BLOCK, (m + 1) * BLOCK)
            acc[0, names[m]] += grad_keys[rows]
            acc[1, names[m]] += grad_values[rows]
    dkv_ref[...] = acc[...].astype(jnp.bfloat16)


def local_grads(tiles, kinds, kv, qh, gh):
    pair = pl.BlockSpec((2, TILES, BLOCK, HEAD), lambda h, *_: (h, 0, 0, 0))
    heads = pl.BlockSpec((4, BLOCK, 2 * HEAD), lambda h, *_: (0, 0, h))
    return pl.pallas_call(
        grads_kernel,
        name="local_grads",
        out_shape=(
            jax.ShapeDtypeStruct((UNITS, TILES, BLOCK, HEAD), jnp.bfloat16),
            jax.ShapeDtypeStruct((4, BLOCK, 1024), jnp.bfloat16),
        ),
        grid_spec=pltpu.PrefetchScalarGridSpec(
            num_scalar_prefetch=2,
            grid=(HEADS,),
            in_specs=[pair, heads, heads],
            out_specs=(pair, heads),
            scratch_shapes=[pltpu.VMEM((2, TILES, BLOCK, HEAD), jnp.float32)],
        ),
        compiler_params=pltpu.CompilerParams(vmem_limit_bytes=32 << 20),
    )(tiles, kinds, kv, qh, gh)


def scatter_kernel(
    dkv_ref, dq_ref, oq_ref, ok_ref, ov_ref,
    part, near, mid, back, summed, relay, total,
    xs, xr, qs, qr, s1, r1, s2, r2, s3, r3, sp, rp, local,
):
    tm, core, x, z_hi, z = place()
    right, left, far_right, far_left, partner, along_x = ring_peers()
    from_left = lax.div(lax.rem(z + 7, 8), 4)
    from_far = 1 - from_left
    opposite = 1 - z_hi
    meet([right, left, far_right, far_left, partner] + along_x)
    order = X_ORDER
    f32, bf16 = jnp.float32, jnp.bfloat16

    waits = []
    across = {}
    for unit in order:
        across[unit] = send(dkv_ref.at[unit, pl.ds(8, 8)], part.at[unit], (sp, rp), unit, partner)
    q_copies = []
    for d in (1, 2, 3):
        q_copies.append(
            send(dq_ref.at[lax.rem(x + d, 4)], oq_ref.at[:, columns(x * 1024, 1024)],
                 (qs, qr), d - 1, along_x[d - 1])
        )
    own_q = pltpu.make_async_copy(
        dq_ref.at[x], oq_ref.at[:, columns(x * 1024, 1024)], local.at[UNITS]
    )
    own_q.start()

    def quad(kept, half):
        return pl.ds(kept * 8 + half * 4, 4)

    def add(*terms):
        out = terms[0].astype(f32)
        for term in terms[1:]:
            out = out + term.astype(f32)
        return out.astype(bf16)

    first, second, third = {}, {}, {}
    for unit in order:
        across[unit].wait_recv()
        summed[unit, pl.ds(core * 8, 8)] = add(dkv_ref[unit, pl.ds(core * 16, 8)], part[unit])
        summed[unit, pl.ds(8 - core * 8, 8)] = dkv_ref[unit, pl.ds(16 - core * 16, 8)]
        if unit in PLUS:
            piece = summed.at[unit, quad(1, from_far)]
            first[unit] = send(piece, near.at[unit], (s1, r1), unit, left)
        else:
            piece = summed.at[unit, quad(0, opposite)]
            first[unit] = send(piece, near.at[unit], (s1, r1), unit, right)
    for unit in order:
        first[unit].wait_recv()
        if unit in PLUS:
            relay[unit] = add(near[unit], summed[unit, quad(0, opposite)])
            second[unit] = send(relay.at[unit], mid.at[unit], (s2, r2), unit, far_right)
        else:
            relay[unit] = add(near[unit], summed[unit, quad(1, from_far)])
            second[unit] = send(relay.at[unit], mid.at[unit], (s2, r2), unit, far_left)
            piece = summed.at[unit, quad(1, from_left)]
            third[unit] = send(piece, back.at[unit], (s3, r3), unit, left)
    passed = {}
    for unit in PLUS:
        second[unit].wait_recv()
        first[unit].wait_send()
        total[unit] = add(mid[unit], summed[unit, quad(1, from_left)])
        third[unit] = send(total.at[unit], back.at[unit], (s3, r3), unit, left)

    x_copies = []

    def finish(unit):
        third[unit].wait_recv()
        if unit in PLUS:
            third[unit].wait_send()
            total[unit] = add(summed[unit, quad(0, z_hi)], back[unit])
        else:
            second[unit].wait_recv()
            total[unit] = add(summed[unit, quad(0, z_hi)], mid[unit], back[unit])
        ref = ov_ref if unit % 2 else ok_ref
        place_there = columns((x * HEADS + unit // 2) * HEAD, HEAD)
        for d in (1, 2, 3):
            x_copies.append(
                send(total.at[unit, lax.rem(x + d, 4)], ref.at[:, place_there],
                     (xs, xr), unit * 3 + d - 1, along_x[d - 1])
            )
        own = pltpu.make_async_copy(total.at[unit, x], ref.at[:, place_there], local.at[unit])
        own.start()
        return own

    owns = [own_q] + [finish(unit) for unit in MINUS + PLUS]
    for copy in q_copies + x_copies:
        copy.wait_recv()
    for own in owns:
        own.wait()
    for unit in range(UNITS):
        across[unit].wait_send()
        second[unit].wait_send()
        if unit not in PLUS:
            first[unit].wait_send()
            third[unit].wait_send()
    for copy in q_copies + x_copies:
        copy.wait_send()


def scatter(dkv, dq):
    spec = pl.BlockSpec(memory_space=pltpu.VMEM)
    dma = pltpu.SemaphoreType.DMA
    unit = pltpu.VMEM((UNITS, 4, BLOCK, HEAD), jnp.bfloat16)
    return pl.pallas_call(
        scatter_kernel,
        name="scatter_heads",
        out_shape=(
            jax.ShapeDtypeStruct((BLOCK, 4096), jnp.bfloat16),
            jax.ShapeDtypeStruct((BLOCK, 2048), jnp.bfloat16),
            jax.ShapeDtypeStruct((BLOCK, 2048), jnp.bfloat16),
        ),
        in_specs=[spec] * 2,
        out_specs=(spec,) * 3,
        scratch_shapes=[
            pltpu.VMEM((UNITS, 8, BLOCK, HEAD), jnp.bfloat16),
            unit,
            unit,
            unit,
            pltpu.VMEM((UNITS, 16, BLOCK, HEAD), jnp.bfloat16),
            unit,
            unit,
        ]
        + [dma((24,)), dma((24,)), dma((3,)), dma((3,))]
        + [dma((UNITS,))] * 8
        + [dma((UNITS + 1,))],
        compiler_params=pltpu.CompilerParams(
            collective_id=2, has_side_effects=True, vmem_limit_bytes=32 << 20
        ),
    )(dkv, dq)


def body(queries, keys, values, output_gradient, tiles, kinds):
    kv, qh, gh = gather(queries, keys, values, output_gradient)
    dkv, dq = local_grads(tiles, kinds, kv, qh, gh)
    return scatter(dkv, dq)


def solution(mesh):
    rows = P(("tm", "space"), None)
    return jax.shard_map(
        body,
        mesh=mesh,
        in_specs=(rows, rows, rows, rows, P("tm", None), P("tm", None)),
        out_specs=(rows, rows, rows),
        check_vma=False,
    )
```

```python
import functools

import jax
import jax.numpy as jnp
from jax import lax
from jax.experimental import pallas as pl
from jax.experimental.pallas import tpu as pltpu
from jax.sharding import PartitionSpec as P

HEAD = 128
BLOCK = 128
MAXT = 6
HEADS = 4
UNITS = 2 * HEADS
TILES = 24
PLUS = (1, 4, 6)
MESH = pl.DeviceIdType.MESH
LOG2E = 1.4426950408889634


def place():
    tm = lax.axis_index("tm")
    space = lax.axis_index("space")
    core = lax.rem(tm, 2)
    z_lo = lax.rem(lax.div(tm, 2), 4)
    x = lax.rem(space, 4)
    z_hi = lax.div(space, 4)
    return tm, core, x, z_hi, z_hi * 4 + z_lo


def ring_peers():
    tm, core, x, z_hi, z = place()

    def at(tm_step, z_step):
        there = lax.rem(z + z_step, 8)
        return {"tm": lax.rem(tm + tm_step, 32), "space": lax.div(there, 4) * 4 + x}

    right, left, far_right, far_left = at(2, 1), at(30, 7), at(2, 5), at(30, 3)
    partner = {"tm": tm + 1 - 2 * core, "space": z_hi * 4 + x}
    along_x = [{"tm": tm, "space": z_hi * 4 + lax.rem(x + d, 4)} for d in (1, 2, 3)]
    return right, left, far_right, far_left, partner, along_x


def meet(peers):
    barrier = pltpu.get_barrier_semaphore()
    for peer in peers:
        pl.semaphore_signal(barrier, inc=1, device_id=peer, device_id_type=MESH)
    pl.semaphore_wait(barrier, len(peers))


def send(src, dst, sems, index, device):
    send_sem, recv_sem = sems
    copy = pltpu.make_async_remote_copy(
        src_ref=src,
        dst_ref=dst,
        send_sem=send_sem.at[index],
        recv_sem=recv_sem.at[index],
        device_id=device,
        device_id_type=MESH,
    )
    copy.start()
    return copy


def columns(start, width):
    return pl.ds(pl.multiple_of(start, width), width)


NT = (((1,), (1,)), ((), ()))
NN = (((1,), (0,)), ((), ()))
TN = (((0,), (0,)), ((), ()))


def dot(a, b, dims):
    return lax.dot_general(a, b, dims, preferred_element_type=jnp.float32)


def add(*terms):
    out = terms[0].astype(jnp.float32)
    for term in terms[1:]:
        out = out + term.astype(jnp.float32)
    return out.astype(jnp.bfloat16)


def head_grads(h, half, tiles_ref, kinds_ref, kv_ref, q_ref, g_ref, slots, dq_ref):
    scale = 1.0 / HEAD**0.5
    row = lax.broadcasted_iota(jnp.int32, (BLOCK, 2 * BLOCK), 0)
    col = lax.broadcasted_iota(jnp.int32, (BLOCK, 2 * BLOCK), 1)
    ahead = row - jnp.where(col >= BLOCK, col - BLOCK, col)
    one, two = pl.ds(h * 256, HEAD), pl.ds(h * 256 + HEAD, HEAD)

    def block(b, carry):
        line = half * 4 + b
        names = [tiles_ref[line, m] for m in range(MAXT)]
        kinds = [kinds_ref[line, m] for m in range(MAXT)]
        k = jnp.concatenate([kv_ref[0, t] for t in names], axis=0)
        v = jnp.concatenate([kv_ref[1, t] for t in names], axis=0)
        q = jnp.concatenate([q_ref[b, :, one], q_ref[b, :, two]], axis=0)
        g = jnp.concatenate([g_ref[b, :, one], g_ref[b, :, two]], axis=0)
        scores = dot(k, q, NT)
        masked = []
        for m in range(MAXT):
            limit = jnp.where(kinds[m] == 0, BLOCK, jnp.where(kinds[m] == 1, 0, -2 * BLOCK))
            masked.append(
                jnp.where(ahead <= limit, scores[m * BLOCK : (m + 1) * BLOCK], -jnp.inf)
            )
        scores = jnp.concatenate(masked, axis=0)
        top = jnp.max(scores, axis=0, keepdims=True)
        weights = jnp.exp2((scores - top) * (scale * LOG2E))
        probs = weights * (1.0 / jnp.sum(weights, axis=0, keepdims=True))
        low = probs.astype(jnp.bfloat16)
        grad_probs = dot(v, g, NT)
        delta = jnp.sum(low.astype(jnp.float32) * grad_probs, axis=0, keepdims=True)
        grad_scores = (probs * (grad_probs - delta) * scale).astype(jnp.bfloat16)
        slots[1, b, :MAXT] = dot(low, g, NN).reshape(MAXT, BLOCK, HEAD)
        slots[0, b, :MAXT] = dot(grad_scores, q, NN).reshape(MAXT, BLOCK, HEAD)
        grad_q = dot(grad_scores, k, TN).astype(jnp.bfloat16)
        dq_ref[b, :, one] = grad_q[:BLOCK]
        dq_ref[b, :, two] = grad_q[BLOCK:]
        return carry

    lax.fori_loop(0, 4, block, 0)


def kernel(
    tiles_ref, kinds_ref, q_in, k_in, v_in, g_in, oq_ref, ok_ref, ov_ref,
    kv0, kv1, kv2, kv3, qh, gh, dq, slots, where, dkv,
    part, near, mid, back, summed, relay, total,
    xs, xr, qs, qr, s1, r1, s2, r2, s3, r3, sp, rp,
    os_, or_, ys, yr, t1, u1, t2, u2, t3, u3, tp, up, local, local_out,
):
    tm, core, x, z_hi, z = place()
    right, left, far_right, far_left, partner, along_x = ring_peers()
    from_left = lax.div(lax.rem(z + 7, 8), 4)
    from_far = 1 - from_left
    opposite = 1 - z_hi
    kv = (kv0, kv1, kv2, kv3)
    meet([right, left, far_right, far_left, partner] + along_x)

    def quad(window, half):
        return pl.ds(window * 8 + half * 4, 4)

    def buffer(unit):
        return kv[unit // 2].at[unit % 2]

    def source(unit, to_x):
        ref = v_in if unit % 2 else k_in
        return ref.at[:, columns((to_x * HEADS + unit // 2) * HEAD, HEAD)]

    def units(h):
        return (2 * h, 2 * h + 1)

    x_copies, own, q_copies = {}, {}, {}
    first, second, third, across = {}, {}, {}, {}
    out_q, out_x, own_out = [], [], []
    near_c, far_c, back_c, across_out = {}, {}, {}, {}

    def spread(h):
        for unit in units(h):
            there = buffer(unit).at[z_hi * 4 + x]
            x_copies[unit] = [
                send(source(unit, lax.rem(x + d, 4)), there, (xs, xr), unit * 3 + d - 1,
                     along_x[d - 1])
                for d in (1, 2, 3)
            ]
            own[unit] = pltpu.make_async_copy(source(unit, x), there, local.at[unit])
            own[unit].start()

    def spread_q(h):
        q_copies[h] = []
        for i, (ref, to) in enumerate(((q_in, qh), (g_in, gh))):
            there = to.at[x, :, pl.ds(h * 256, 256)]
            for d in (1, 2, 3):
                q_copies[h].append(
                    send(ref.at[:, columns(lax.rem(x + d, 4) * 1024 + h * 256, 256)], there,
                         (qs, qr), h * 6 + i * 3 + d - 1, along_x[d - 1])
                )
            mine = pltpu.make_async_copy(
                ref.at[:, columns(x * 1024 + h * 256, 256)], there,
                local.at[UNITS + 2 * h + i])
            mine.start()
            own[UNITS + 2 * h + i] = mine

    def start(h):
        for unit in units(h):
            own[unit].wait()
            for copy in x_copies[unit]:
                copy.wait_recv()
            piece = buffer(unit).at[quad(0, z_hi)]
            there = buffer(unit).at[quad(2, z_hi)]
            if unit not in PLUS:
                second[unit] = send(piece, there, (s2, r2), unit, far_right)
            first[unit] = send(piece, there, (s1, r1), unit, right)

    def hop(h):
        for unit in units(h):
            buf = buffer(unit)
            if unit in PLUS:
                first[unit].wait_recv()
                second[unit] = send(buf.at[quad(2, from_left)], buf.at[quad(0, from_left)],
                                    (s2, r2), unit, far_left)
            else:
                second[unit].wait_recv()
                third[unit] = send(buf.at[quad(2, from_far)], buf.at[quad(0, from_far)],
                                   (s3, r3), unit, left)

    def last_hop(h):
        for unit in units(h):
            if unit in PLUS:
                buf = buffer(unit)
                second[unit].wait_recv()
                third[unit] = send(buf.at[quad(0, opposite)], buf.at[quad(2, opposite)],
                                   (s3, r3), unit, right)

    def share(h):
        for unit in units(h):
            buf = buffer(unit)
            if unit not in PLUS:
                first[unit].wait_recv()
            third[unit].wait_recv()
            across[unit] = send(buf.at[pl.ds(core * 16, 8)], buf.at[pl.ds(8, 8)],
                                (sp, rp), unit, partner)

    def compute(h):
        for unit in units(h):
            across[unit].wait_recv()
        for copy in q_copies[h]:
            copy.wait_recv()
        own[UNITS + 2 * h].wait()
        own[UNITS + 2 * h + 1].wait()
        head_grads(h, z_hi, tiles_ref, kinds_ref, kv[h], qh, gh, slots, dq)

        def tile(t, carry):
            for i in (0, 1):
                terms = [slots[i, b, where[b * TILES + t]] for b in range(4)]
                dkv[2 * h + i, t] = ((terms[0] + terms[1]) + (terms[2] + terms[3])).astype(
                    jnp.bfloat16
                )
            return carry

        lax.fori_loop(0, TILES, tile, 0)
        for unit in units(h):
            across_out[unit] = send(dkv.at[unit, pl.ds(8, 8)], part.at[unit], (tp, up), unit,
                                    partner)
        there = oq_ref.at[:, columns(x * 1024 + h * 256, 256)]
        for d in (1, 2, 3):
            out_q.append(
                send(dq.at[lax.rem(x + d, 4), :, pl.ds(h * 256, 256)], there, (os_, or_),
                     h * 3 + d - 1, along_x[d - 1])
            )
        mine = pltpu.make_async_copy(dq.at[x, :, pl.ds(h * 256, 256)], there,
                                     local_out.at[UNITS + h])
        mine.start()
        own_out.append(mine)

    def fold(h):
        for unit in units(h):
            across_out[unit].wait_recv()
            summed[unit, pl.ds(core * 8, 8)] = add(dkv[unit, pl.ds(core * 16, 8)], part[unit])
            summed[unit, pl.ds(8 - core * 8, 8)] = dkv[unit, pl.ds(16 - core * 16, 8)]
            if unit in PLUS:
                near_c[unit] = send(summed.at[unit, quad(1, from_far)], near.at[unit],
                                    (t1, u1), unit, left)
            else:
                near_c[unit] = send(summed.at[unit, quad(0, opposite)], near.at[unit],
                                    (t1, u1), unit, right)

    def pass_on(h):
        for unit in units(h):
            near_c[unit].wait_recv()
            if unit in PLUS:
                relay[unit] = add(near[unit], summed[unit, quad(0, opposite)])
                far_c[unit] = send(relay.at[unit], mid.at[unit], (t2, u2), unit, far_right)
            else:
                relay[unit] = add(near[unit], summed[unit, quad(1, from_far)])
                far_c[unit] = send(relay.at[unit], mid.at[unit], (t2, u2), unit, far_left)
                back_c[unit] = send(summed.at[unit, quad(1, from_left)], back.at[unit],
                                    (t3, u3), unit, left)

    def turn(h):
        for unit in units(h):
            if unit in PLUS:
                far_c[unit].wait_recv()
                total[unit] = add(mid[unit], summed[unit, quad(1, from_left)])
                back_c[unit] = send(total.at[unit], back.at[unit], (t3, u3), unit, left)

    def finish(h):
        for unit in units(h):
            back_c[unit].wait_recv()
            if unit in PLUS:
                back_c[unit].wait_send()
                total[unit] = add(summed[unit, quad(0, z_hi)], back[unit])
            else:
                far_c[unit].wait_recv()
                total[unit] = add(summed[unit, quad(0, z_hi)], mid[unit], back[unit])
            ref = ov_ref if unit % 2 else ok_ref
            there = ref.at[:, columns((x * HEADS + unit // 2) * HEAD, HEAD)]
            for d in (1, 2, 3):
                out_x.append(
                    send(total.at[unit, lax.rem(x + d, 4)], there, (ys, yr), unit * 3 + d - 1,
                         along_x[d - 1])
                )
            mine = pltpu.make_async_copy(total.at[unit, x], there, local_out.at[unit])
            mine.start()
            own_out.append(mine)

    def find_slots():
        def one(t, carry):
            for b in range(4):
                found = MAXT
                for m in reversed(range(MAXT)):
                    found = jnp.where(tiles_ref[z_hi * 4 + b, m] == t, m, found)
                where[b * TILES + t] = found
            return carry

        lax.fori_loop(0, TILES, one, 0)
        for i in (0, 1):
            for b in range(4):
                slots[i, b, MAXT] = jnp.zeros((BLOCK, HEAD), jnp.float32)

    for step, h in ((spread, 0), (spread, 1), (spread_q, 0), (spread, 2), (spread_q, 1),
                    (spread, 3), (spread_q, 2), (spread_q, 3)):
        step(h)
    start(0)
    start(1)
    find_slots()
    for step, h in ORDER:
        {"start": start, "hop": hop, "last_hop": last_hop, "share": share, "compute": compute,
         "fold": fold, "pass_on": pass_on, "turn": turn, "finish": finish}[step](h)

    for copy in out_q + out_x:
        copy.wait_recv()
    for mine in own_out:
        mine.wait()
    sent = [c for table in (x_copies, q_copies) for copies in table.values() for c in copies]
    for table in (first, second, third, across, near_c, far_c, across_out):
        sent += list(table.values())
    sent += [back_c[unit] for unit in range(UNITS) if unit not in PLUS] + out_q + out_x
    for copy in sent:
        copy.wait_send()


ORDER = (
    ("hop", 0), ("start", 2), ("last_hop", 0), ("hop", 1), ("share", 0),
    ("compute", 0),
    ("start", 3), ("last_hop", 1), ("hop", 2), ("share", 1), ("fold", 0),
    ("compute", 1),
    ("pass_on", 0), ("last_hop", 2), ("hop", 3), ("share", 2), ("fold", 1),
    ("compute", 2),
    ("turn", 0), ("pass_on", 1), ("last_hop", 3), ("share", 3), ("fold", 2),
    ("compute", 3),
    ("finish", 0), ("turn", 1), ("pass_on", 2), ("fold", 3),
    ("finish", 1), ("turn", 2), ("pass_on", 3),
    ("finish", 2), ("turn", 3), ("finish", 3),
)


def body(queries, keys, values, output_gradient, tiles, kinds):
    vmem = pl.BlockSpec(memory_space=pltpu.VMEM)
    smem = pl.BlockSpec(memory_space=pltpu.SMEM)
    anywhere = pl.BlockSpec(memory_space=pl.ANY)
    dma = pltpu.SemaphoreType.DMA
    bf16 = jnp.bfloat16
    unit = pltpu.VMEM((UNITS, 4, BLOCK, HEAD), bf16)
    rows = pltpu.VMEM((4, BLOCK, 1024), bf16)
    return pl.pallas_call(
        kernel,
        name="attention_grads",
        out_shape=(
            jax.ShapeDtypeStruct((BLOCK, 4096), bf16),
            jax.ShapeDtypeStruct((BLOCK, 2048), bf16),
            jax.ShapeDtypeStruct((BLOCK, 2048), bf16),
        ),
        in_specs=[smem, smem] + [anywhere] * 4,
        out_specs=(vmem,) * 3,
        scratch_shapes=[pltpu.VMEM((2, TILES, BLOCK, HEAD), bf16)] * HEADS
        + [rows] * 3
        + [
            pltpu.VMEM((2, 4, MAXT + 1, BLOCK, HEAD), jnp.float32),
            pltpu.SMEM((4 * TILES,), jnp.int32),
            pltpu.VMEM((UNITS, TILES, BLOCK, HEAD), bf16),
            pltpu.VMEM((UNITS, 8, BLOCK, HEAD), bf16),
            unit,
            unit,
            unit,
            pltpu.VMEM((UNITS, 16, BLOCK, HEAD), bf16),
            unit,
            unit,
        ]
        + [dma((24,))] * 4
        + [dma((UNITS,))] * 8
        + [dma((12,))] * 2
        + [dma((24,))] * 2
        + [dma((UNITS,))] * 8
        + [dma((2 * UNITS,)), dma((UNITS + HEADS,))],
        compiler_params=pltpu.CompilerParams(
            collective_id=1, has_side_effects=True, vmem_limit_bytes=60 << 20
        ),
    )(tiles, kinds, queries, keys, values, output_gradient)


def solution(mesh):
    rows = P(("tm", "space"), None)
    return jax.shard_map(
        body,
        mesh=mesh,
        in_specs=(rows, rows, rows, rows, P("tm", None), P("tm", None)),
        out_specs=(rows, rows, rows),
        check_vma=False,
    )
```

```python
import functools

import jax
import jax.numpy as jnp
from jax import lax
from jax.experimental import pallas as pl
from jax.experimental.pallas import tpu as pltpu
from jax.sharding import PartitionSpec as P

HEAD = 128
BLOCK = 128
MAXT = 6
HEADS = 4
UNITS = 2 * HEADS
TILES = 24
PLUS = (1, 4, 6)
OUT_PLUS = (1, 4, 6)
MESH = pl.DeviceIdType.MESH
LOG2E = 1.4426950408889634


def place():
    tm = lax.axis_index("tm")
    space = lax.axis_index("space")
    core = lax.rem(tm, 2)
    z_lo = lax.rem(lax.div(tm, 2), 4)
    x = lax.rem(space, 4)
    z_hi = lax.div(space, 4)
    return tm, core, x, z_hi, z_hi * 4 + z_lo


def ring_peers():
    tm, core, x, z_hi, z = place()

    def at(tm_step, z_step):
        there = lax.rem(z + z_step, 8)
        return {"tm": lax.rem(tm + tm_step, 32), "space": lax.div(there, 4) * 4 + x}

    right, left, far_right, far_left = at(2, 1), at(30, 7), at(2, 5), at(30, 3)
    partner = {"tm": tm + 1 - 2 * core, "space": z_hi * 4 + x}
    along_x = [{"tm": tm, "space": z_hi * 4 + lax.rem(x + d, 4)} for d in (1, 2, 3)]
    return right, left, far_right, far_left, partner, along_x


def meet(peers):
    barrier = pltpu.get_barrier_semaphore()
    for peer in peers:
        pl.semaphore_signal(barrier, inc=1, device_id=peer, device_id_type=MESH)
    pl.semaphore_wait(barrier, len(peers))


def send(src, dst, sems, index, device):
    send_sem, recv_sem = sems
    copy = pltpu.make_async_remote_copy(
        src_ref=src,
        dst_ref=dst,
        send_sem=send_sem.at[index],
        recv_sem=recv_sem.at[index],
        device_id=device,
        device_id_type=MESH,
    )
    copy.start()
    return copy


def columns(start, width):
    return pl.ds(pl.multiple_of(start, width), width)


NT = (((1,), (1,)), ((), ()))
NN = (((1,), (0,)), ((), ()))
TN = (((0,), (0,)), ((), ()))


def dot(a, b, dims):
    return lax.dot_general(a, b, dims, preferred_element_type=jnp.float32)


def add(*terms):
    out = terms[0].astype(jnp.float32)
    for term in terms[1:]:
        out = out + term.astype(jnp.float32)
    return out.astype(jnp.bfloat16)


def head_grads(h, half, tiles_ref, kinds_ref, kv_ref, q_ref, g_ref, slots, dq_ref):
    scale = 1.0 / HEAD**0.5
    row = lax.broadcasted_iota(jnp.int32, (BLOCK, 2 * BLOCK), 0)
    col = lax.broadcasted_iota(jnp.int32, (BLOCK, 2 * BLOCK), 1)
    ahead = row - jnp.where(col >= BLOCK, col - BLOCK, col)
    one, two = pl.ds(h * 256, HEAD), pl.ds(h * 256 + HEAD, HEAD)

    def block(b, carry):
        line = half * 4 + b
        names = [tiles_ref[line, m] for m in range(MAXT)]
        kinds = [kinds_ref[line, m] for m in range(MAXT)]
        k = jnp.concatenate([kv_ref[0, t] for t in names], axis=0)
        v = jnp.concatenate([kv_ref[1, t] for t in names], axis=0)
        q = jnp.concatenate([q_ref[b, :, one], q_ref[b, :, two]], axis=0)
        g = jnp.concatenate([g_ref[b, :, one], g_ref[b, :, two]], axis=0)
        scores = dot(k, q, NT)
        masked = []
        for m in range(MAXT):
            limit = jnp.where(kinds[m] == 0, BLOCK, jnp.where(kinds[m] == 1, 0, -2 * BLOCK))
            masked.append(
                jnp.where(ahead <= limit, scores[m * BLOCK : (m + 1) * BLOCK], -jnp.inf)
            )
        scores = jnp.concatenate(masked, axis=0)
        top = jnp.max(scores, axis=0, keepdims=True)
        weights = jnp.exp2((scores - top) * (scale * LOG2E))
        probs = weights * (1.0 / jnp.sum(weights, axis=0, keepdims=True))
        low = probs.astype(jnp.bfloat16)
        grad_probs = dot(v, g, NT)
        delta = jnp.sum(low.astype(jnp.float32) * grad_probs, axis=0, keepdims=True)
        grad_scores = (probs * (grad_probs - delta) * scale).astype(jnp.bfloat16)
        slots[1, b, :MAXT] = dot(low, g, NN).reshape(MAXT, BLOCK, HEAD)
        slots[0, b, :MAXT] = dot(grad_scores, q, NN).reshape(MAXT, BLOCK, HEAD)
        grad_q = dot(grad_scores, k, TN).astype(jnp.bfloat16)
        dq_ref[b, :, one] = grad_q[:BLOCK]
        dq_ref[b, :, two] = grad_q[BLOCK:]
        return carry

    lax.fori_loop(0, 4, block, 0)


def kernel(
    tiles_ref, kinds_ref, q_in, k_in, v_in, g_in, oq_ref, ok_ref, ov_ref,
    kv0, kv1, kv2, kv3, qh, gh, dq, slots, where, dkv,
    part, near, mid, back, summed, relay, total,
    xs, xr, qs, qr, s1, r1, s2, r2, s3, r3, sp, rp,
    os_, or_, ys, yr, t1, u1, t2, u2, t3, u3, tp, up, local, local_out,
):
    tm, core, x, z_hi, z = place()
    right, left, far_right, far_left, partner, along_x = ring_peers()
    from_left = lax.div(lax.rem(z + 7, 8), 4)
    from_far = 1 - from_left
    opposite = 1 - z_hi
    kv = (kv0, kv1, kv2, kv3)
    meet([right, left, far_right, far_left, partner] + along_x)

    def quad(window, half):
        return pl.ds(window * 8 + half * 4, 4)

    def buffer(unit):
        return kv[unit // 2].at[unit % 2]

    def source(unit, to_x):
        ref = v_in if unit % 2 else k_in
        return ref.at[:, columns((to_x * HEADS + unit // 2) * HEAD, HEAD)]

    x_copies, own, q_copies = {}, {}, {}
    first, second, third, across = {}, {}, {}, {}
    out_q, out_x, own_out = [], [], []
    near_c, far_c, back_c, across_out = {}, {}, {}, {}

    def spread(h):
        for unit in (2 * h, 2 * h + 1):
            there = buffer(unit).at[z_hi * 4 + x]
            x_copies[unit] = [
                send(source(unit, lax.rem(x + d, 4)), there, (xs, xr), unit * 3 + d - 1,
                     along_x[d - 1])
                for d in (1, 2, 3)
            ]
            own[unit] = pltpu.make_async_copy(source(unit, x), there, local.at[unit])
            own[unit].start()

    def spread_q(h):
        q_copies[h] = []
        for i, (ref, to) in enumerate(((q_in, qh), (g_in, gh))):
            there = to.at[x, :, pl.ds(h * 256, 256)]
            for d in (1, 2, 3):
                q_copies[h].append(
                    send(ref.at[:, columns(lax.rem(x + d, 4) * 1024 + h * 256, 256)], there,
                         (qs, qr), h * 6 + i * 3 + d - 1, along_x[d - 1])
                )
            mine = pltpu.make_async_copy(
                ref.at[:, columns(x * 1024 + h * 256, 256)], there,
                local.at[UNITS + 2 * h + i])
            mine.start()
            own[UNITS + 2 * h + i] = mine

    def arrive(unit):
        if unit not in arrived:
            own[unit].wait()
            for copy in x_copies[unit]:
                copy.wait_recv()
            arrived.add(unit)

    def begin(unit):
        arrive(unit)
        if unit in PLUS:
            to_right(unit)
        else:
            second[unit] = send(buffer(unit).at[quad(0, z_hi)], buffer(unit).at[quad(2, z_hi)],
                                (s2, r2), unit, far_right)

    def to_right(unit):
        arrive(unit)
        first[unit] = send(buffer(unit).at[quad(0, z_hi)], buffer(unit).at[quad(2, z_hi)],
                           (s1, r1), unit, right)

    def hop(unit):
        buf = buffer(unit)
        if unit in PLUS:
            first[unit].wait_recv()
            second[unit] = send(buf.at[quad(2, from_left)], buf.at[quad(0, from_left)],
                                (s2, r2), unit, far_left)
        else:
            second[unit].wait_recv()
            third[unit] = send(buf.at[quad(2, from_far)], buf.at[quad(0, from_far)],
                               (s3, r3), unit, left)

    def last_hop(unit):
        buf = buffer(unit)
        second[unit].wait_recv()
        third[unit] = send(buf.at[quad(0, opposite)], buf.at[quad(2, opposite)],
                           (s3, r3), unit, right)

    def share(unit):
        buf = buffer(unit)
        if unit not in PLUS:
            first[unit].wait_recv()
        third[unit].wait_recv()
        across[unit] = send(buf.at[pl.ds(core * 16, 8)], buf.at[pl.ds(8, 8)],
                            (sp, rp), unit, partner)

    def compute(h):
        for unit in (2 * h, 2 * h + 1):
            across[unit].wait_recv()
        for copy in q_copies[h]:
            copy.wait_recv()
        own[UNITS + 2 * h].wait()
        own[UNITS + 2 * h + 1].wait()
        head_grads(h, z_hi, tiles_ref, kinds_ref, kv[h], qh, gh, slots, dq)

        def tile(t, carry):
            for i in (0, 1):
                terms = [slots[i, b, where[b * TILES + t]] for b in range(4)]
                dkv[2 * h + i, t] = ((terms[0] + terms[1]) + (terms[2] + terms[3])).astype(
                    jnp.bfloat16
                )
            return carry

        lax.fori_loop(0, TILES, tile, 0)
        for unit in (2 * h, 2 * h + 1):
            across_out[unit] = send(dkv.at[unit, pl.ds(8, 8)], part.at[unit], (tp, up), unit,
                                    partner)
        there = oq_ref.at[:, columns(x * 1024 + h * 256, 256)]
        for d in (1, 2, 3):
            out_q.append(
                send(dq.at[lax.rem(x + d, 4), :, pl.ds(h * 256, 256)], there, (os_, or_),
                     h * 3 + d - 1, along_x[d - 1])
            )
        mine = pltpu.make_async_copy(dq.at[x, :, pl.ds(h * 256, 256)], there,
                                     local_out.at[UNITS + h])
        mine.start()
        own_out.append(mine)

    def fold(unit):
        across_out[unit].wait_recv()
        summed[unit, pl.ds(core * 8, 8)] = add(dkv[unit, pl.ds(core * 16, 8)], part[unit])
        summed[unit, pl.ds(8 - core * 8, 8)] = dkv[unit, pl.ds(16 - core * 16, 8)]
        if unit in OUT_PLUS:
            near_c[unit] = send(summed.at[unit, quad(1, from_far)], near.at[unit],
                                (t1, u1), unit, left)
        else:
            near_c[unit] = send(summed.at[unit, quad(0, opposite)], near.at[unit],
                                (t1, u1), unit, right)

    def give_back(unit):
        back_c[unit] = send(summed.at[unit, quad(1, from_left)], back.at[unit],
                            (t3, u3), unit, left)

    def pass_on(unit):
        near_c[unit].wait_recv()
        if unit in OUT_PLUS:
            relay[unit] = add(near[unit], summed[unit, quad(0, opposite)])
            far_c[unit] = send(relay.at[unit], mid.at[unit], (t2, u2), unit, far_right)
        else:
            relay[unit] = add(near[unit], summed[unit, quad(1, from_far)])
            far_c[unit] = send(relay.at[unit], mid.at[unit], (t2, u2), unit, far_left)

    def turn(unit):
        far_c[unit].wait_recv()
        total[unit] = add(mid[unit], summed[unit, quad(1, from_left)])
        back_c[unit] = send(total.at[unit], back.at[unit], (t3, u3), unit, left)

    def finish(unit):
        back_c[unit].wait_recv()
        if unit in OUT_PLUS:
            back_c[unit].wait_send()
            total[unit] = add(summed[unit, quad(0, z_hi)], back[unit])
        else:
            far_c[unit].wait_recv()
            total[unit] = add(summed[unit, quad(0, z_hi)], mid[unit], back[unit])
        ref = ov_ref if unit % 2 else ok_ref
        there = ref.at[:, columns((x * HEADS + unit // 2) * HEAD, HEAD)]
        for d in (1, 2, 3):
            out_x.append(
                send(total.at[unit, lax.rem(x + d, 4)], there, (ys, yr), unit * 3 + d - 1,
                     along_x[d - 1])
            )
        mine = pltpu.make_async_copy(total.at[unit, x], there, local_out.at[unit])
        mine.start()
        own_out.append(mine)

    def find_slots(_):
        def one(t, carry):
            for b in range(4):
                found = MAXT
                for m in reversed(range(MAXT)):
                    found = jnp.where(tiles_ref[z_hi * 4 + b, m] == t, m, found)
                where[b * TILES + t] = found
            return carry

        lax.fori_loop(0, TILES, one, 0)
        for i in (0, 1):
            for b in range(4):
                slots[i, b, MAXT] = jnp.zeros((BLOCK, HEAD), jnp.float32)

    arrived = set()
    steps = {"X": spread, "Q": spread_q, "a": begin, "b": to_right, "c": hop, "d": share,
             "e": last_hop, "K": compute, "f": fold, "g": give_back, "p": pass_on, "t": turn,
             "y": finish, "w": find_slots}
    for name in ORDER:
        steps[name[0]](int(name[1]))

    for copy in out_q + out_x:
        copy.wait_recv()
    for mine in own_out:
        mine.wait()
    sent = [c for table in (x_copies, q_copies) for copies in table.values() for c in copies]
    for table in (first, second, third, across, near_c, far_c, across_out):
        sent += list(table.values())
    sent += [back_c[unit] for unit in range(UNITS) if unit not in OUT_PLUS] + out_q + out_x
    for copy in sent:
        copy.wait_send()


ORDER = (
    "X0", "X1", "X2", "X3", "b0", "a0", "a1", "w0", "b2", "a2", "b3", "a4",
    "Q0", "c1", "a3", "Q1", "c0", "a6", "c4", "Q2", "c2", "Q3", "a5", "e1",
    "c6", "c3", "d0", "d2", "a7", "e4", "d1", "K0", "d3", "b5", "c5", "b7",
    "f0", "g0", "e6", "f1", "d4", "K1", "c7", "d5", "f2", "g2", "p0", "f3",
    "g3", "K2", "p1", "p2", "d6", "d7", "f4", "f5", "K3", "y0", "p3", "g5",
    "f6", "f7", "g7", "t1", "p4", "y2", "p5", "p6", "y1", "y3", "p7", "t4",
    "y5", "t6", "y4", "y6", "y7",
)


def body(queries, keys, values, output_gradient, tiles, kinds):
    vmem = pl.BlockSpec(memory_space=pltpu.VMEM)
    smem = pl.BlockSpec(memory_space=pltpu.SMEM)
    anywhere = pl.BlockSpec(memory_space=pl.ANY)
    dma = pltpu.SemaphoreType.DMA
    bf16 = jnp.bfloat16
    unit = pltpu.VMEM((UNITS, 4, BLOCK, HEAD), bf16)
    rows = pltpu.VMEM((4, BLOCK, 1024), bf16)
    return pl.pallas_call(
        kernel,
        name="attention_grads",
        out_shape=(
            jax.ShapeDtypeStruct((BLOCK, 4096), bf16),
            jax.ShapeDtypeStruct((BLOCK, 2048), bf16),
            jax.ShapeDtypeStruct((BLOCK, 2048), bf16),
        ),
        in_specs=[smem, smem] + [anywhere] * 4,
        out_specs=(vmem,) * 3,
        scratch_shapes=[pltpu.VMEM((2, TILES, BLOCK, HEAD), bf16)] * HEADS
        + [rows] * 3
        + [
            pltpu.VMEM((2, 4, MAXT + 1, BLOCK, HEAD), jnp.float32),
            pltpu.SMEM((4 * TILES,), jnp.int32),
            pltpu.VMEM((UNITS, TILES, BLOCK, HEAD), bf16),
            pltpu.VMEM((UNITS, 8, BLOCK, HEAD), bf16),
            unit,
            unit,
            unit,
            pltpu.VMEM((UNITS, 16, BLOCK, HEAD), bf16),
            unit,
            unit,
        ]
        + [dma((24,))] * 4
        + [dma((UNITS,))] * 8
        + [dma((12,))] * 2
        + [dma((24,))] * 2
        + [dma((UNITS,))] * 8
        + [dma((2 * UNITS,)), dma((UNITS + HEADS,))],
        compiler_params=pltpu.CompilerParams(
            collective_id=1, has_side_effects=True, vmem_limit_bytes=60 << 20
        ),
    )(tiles, kinds, queries, keys, values, output_gradient)


def solution(mesh):
    rows = P(("tm", "space"), None)
    return jax.shard_map(
        body,
        mesh=mesh,
        in_specs=(rows, rows, rows, rows, P("tm", None), P("tm", None)),
        out_specs=(rows, rows, rows),
        check_vma=False,
    )
```

```python
import functools

import jax
import jax.numpy as jnp
from jax import lax
from jax.experimental import pallas as pl
from jax.experimental.pallas import tpu as pltpu
from jax.sharding import PartitionSpec as P

HEAD = 128
BLOCK = 128
MAXT = 6
HEADS = 4
UNITS = 2 * HEADS
TILES = 24
PLUS = (1, 4, 6)
OUT_PLUS = (1, 4, 6)
EARLY = (0, 1)
MESH = pl.DeviceIdType.MESH
LOG2E = 1.4426950408889634


def place():
    tm = lax.axis_index("tm")
    space = lax.axis_index("space")
    core = lax.rem(tm, 2)
    z_lo = lax.rem(lax.div(tm, 2), 4)
    x = lax.rem(space, 4)
    z_hi = lax.div(space, 4)
    return tm, core, x, z_hi, z_hi * 4 + z_lo


def ring_peers():
    tm, core, x, z_hi, z = place()

    def at(tm_step, z_step):
        there = lax.rem(z + z_step, 8)
        return {"tm": lax.rem(tm + tm_step, 32), "space": lax.div(there, 4) * 4 + x}

    right, left, far_right, far_left = at(2, 1), at(30, 7), at(2, 5), at(30, 3)
    partner = {"tm": tm + 1 - 2 * core, "space": z_hi * 4 + x}
    along_x = [{"tm": tm, "space": z_hi * 4 + lax.rem(x + d, 4)} for d in (1, 2, 3)]
    return right, left, far_right, far_left, partner, along_x


def meet(peers):
    barrier = pltpu.get_barrier_semaphore()
    for peer in peers:
        pl.semaphore_signal(barrier, inc=1, device_id=peer, device_id_type=MESH)
    pl.semaphore_wait(barrier, len(peers))


def send(src, dst, sems, index, device):
    send_sem, recv_sem = sems
    copy = pltpu.make_async_remote_copy(
        src_ref=src,
        dst_ref=dst,
        send_sem=send_sem.at[index],
        recv_sem=recv_sem.at[index],
        device_id=device,
        device_id_type=MESH,
    )
    copy.start()
    return copy


class Pieces:
    def __init__(self):
        self.copies = []

    def wait_recv(self):
        for copy in self.copies:
            copy.wait_recv()

    def wait_send(self):
        for copy in self.copies:
            copy.wait_send()


def columns(start, width):
    return pl.ds(pl.multiple_of(start, width), width)


NT = (((1,), (1,)), ((), ()))
NN = (((1,), (0,)), ((), ()))
TN = (((0,), (0,)), ((), ()))


def dot(a, b, dims):
    return lax.dot_general(a, b, dims, preferred_element_type=jnp.float32)


def add(*terms):
    out = terms[0].astype(jnp.float32)
    for term in terms[1:]:
        out = out + term.astype(jnp.float32)
    return out.astype(jnp.bfloat16)


def head_grads(h, half, tiles_ref, kinds_ref, kv_ref, q_ref, g_ref, slots, dq_ref):
    scale = 1.0 / HEAD**0.5
    row = lax.broadcasted_iota(jnp.int32, (BLOCK, 2 * BLOCK), 0)
    col = lax.broadcasted_iota(jnp.int32, (BLOCK, 2 * BLOCK), 1)
    ahead = row - jnp.where(col >= BLOCK, col - BLOCK, col)
    one, two = pl.ds(h * 256, HEAD), pl.ds(h * 256 + HEAD, HEAD)

    def block(b, carry):
        line = half * 4 + b
        names = [tiles_ref[line, m] for m in range(MAXT)]
        kinds = [kinds_ref[line, m] for m in range(MAXT)]
        k = jnp.concatenate([kv_ref[0, t] for t in names], axis=0)
        v = jnp.concatenate([kv_ref[1, t] for t in names], axis=0)
        q = jnp.concatenate([q_ref[b, :, one], q_ref[b, :, two]], axis=0)
        g = jnp.concatenate([g_ref[b, :, one], g_ref[b, :, two]], axis=0)
        scores = dot(k, q, NT)
        masked = []
        for m in range(MAXT):
            limit = jnp.where(kinds[m] == 0, BLOCK, jnp.where(kinds[m] == 1, 0, -2 * BLOCK))
            masked.append(
                jnp.where(ahead <= limit, scores[m * BLOCK : (m + 1) * BLOCK], -jnp.inf)
            )
        scores = jnp.concatenate(masked, axis=0)
        top = jnp.max(scores, axis=0, keepdims=True)
        weights = jnp.exp2((scores - top) * (scale * LOG2E))
        probs = weights * (1.0 / jnp.sum(weights, axis=0, keepdims=True))
        low = probs.astype(jnp.bfloat16)
        grad_probs = dot(v, g, NT)
        delta = jnp.sum(low.astype(jnp.float32) * grad_probs, axis=0, keepdims=True)
        grad_scores = (probs * (grad_probs - delta) * scale).astype(jnp.bfloat16)
        slots[1, b, :MAXT] = dot(low, g, NN).reshape(MAXT, BLOCK, HEAD)
        slots[0, b, :MAXT] = dot(grad_scores, q, NN).reshape(MAXT, BLOCK, HEAD)
        grad_q = dot(grad_scores, k, TN).astype(jnp.bfloat16)
        dq_ref[b, :, one] = grad_q[:BLOCK]
        dq_ref[b, :, two] = grad_q[BLOCK:]
        return carry

    lax.fori_loop(0, 4, block, 0)


def kernel(
    tiles_ref, kinds_ref, q_in, k_in, v_in, g_in, oq_ref, ok_ref, ov_ref,
    kv0, kv1, kv2, kv3, qh, gh, dq, slots, where, dkv,
    part, near, mid, back, summed, relay, total,
    xs, xr, qs, qr, s1, r1, s2, r2, s3, r3, sp, rp,
    os_, or_, ys, yr, t1, u1, t2, u2, t3, u3, tp, up, e1s, e1r, e2s, e2r, local, local_out,
):
    tm, core, x, z_hi, z = place()
    right, left, far_right, far_left, partner, along_x = ring_peers()
    from_left = lax.div(lax.rem(z + 7, 8), 4)
    from_far = 1 - from_left
    opposite = 1 - z_hi
    kv = (kv0, kv1, kv2, kv3)
    meet([right, left, far_right, far_left, partner] + along_x)

    def quad(window, half):
        return pl.ds(window * 8 + half * 4, 4)

    def buffer(unit):
        return kv[unit // 2].at[unit % 2]

    def source(unit, to_x):
        ref = v_in if unit % 2 else k_in
        return ref.at[:, columns((to_x * HEADS + unit // 2) * HEAD, HEAD)]

    x_copies, own, q_copies = {}, {}, {}
    first, second, third, across = {}, {}, {}, {}
    out_q, out_x, own_out = [], [], []
    near_c, far_c, back_c, across_out = {}, {}, {}, {}

    def spread(h):
        for unit in (2 * h, 2 * h + 1):
            there = buffer(unit).at[z_hi * 4 + x]
            x_copies[unit] = [
                send(source(unit, lax.rem(x + d, 4)), there, (xs, xr), unit * 3 + d - 1,
                     along_x[d - 1])
                for d in (1, 2, 3)
            ]
            own[unit] = pltpu.make_async_copy(source(unit, x), there, local.at[unit])
            own[unit].start()

    def spread_q(h):
        q_copies[h] = []
        for i, (ref, to) in enumerate(((q_in, qh), (g_in, gh))):
            there = to.at[x, :, pl.ds(h * 256, 256)]
            for d in (1, 2, 3):
                q_copies[h].append(
                    send(ref.at[:, columns(lax.rem(x + d, 4) * 1024 + h * 256, 256)], there,
                         (qs, qr), h * 6 + i * 3 + d - 1, along_x[d - 1])
                )
            mine = pltpu.make_async_copy(
                ref.at[:, columns(x * 1024 + h * 256, 256)], there,
                local.at[UNITS + 2 * h + i])
            mine.start()
            own[UNITS + 2 * h + i] = mine

    def arrive(unit):
        if unit not in arrived:
            own[unit].wait()
            for copy in x_copies[unit]:
                copy.wait_recv()
            arrived.add(unit)

    def begin(unit):
        arrive(unit)
        if unit in PLUS:
            to_right(unit)
        else:
            second[unit] = send(buffer(unit).at[quad(0, z_hi)], buffer(unit).at[quad(2, z_hi)],
                                (s2, r2), unit, far_right)

    def to_right(unit):
        arrive(unit)
        first[unit] = send(buffer(unit).at[quad(0, z_hi)], buffer(unit).at[quad(2, z_hi)],
                           (s1, r1), unit, right)

    for unit in EARLY:
        first[unit] = Pieces()
        if unit not in PLUS:
            second[unit] = Pieces()

    def block_on(unit, step):
        at = z_hi * 4 + lax.rem(x + 4 - step, 4)
        if step:
            x_copies[unit][step - 1].wait_recv()
            piece = buffer(unit).at[at]
        else:
            piece = source(unit, x)
        there = buffer(unit).at[16 + at]
        if unit not in PLUS:
            second[unit].copies.append(
                send(piece, there, (e2s, e2r), unit * 4 + step, far_right))
        first[unit].copies.append(send(piece, there, (e1s, e1r), unit * 4 + step, right))
        if step == 2:
            own[unit].wait()

    def hop(unit):
        buf = buffer(unit)
        if unit in PLUS:
            first[unit].wait_recv()
            second[unit] = send(buf.at[quad(2, from_left)], buf.at[quad(0, from_left)],
                                (s2, r2), unit, far_left)
        else:
            second[unit].wait_recv()
            third[unit] = send(buf.at[quad(2, from_far)], buf.at[quad(0, from_far)],
                               (s3, r3), unit, left)

    def last_hop(unit):
        buf = buffer(unit)
        second[unit].wait_recv()
        third[unit] = send(buf.at[quad(0, opposite)], buf.at[quad(2, opposite)],
                           (s3, r3), unit, right)

    def share(unit):
        buf = buffer(unit)
        if unit not in PLUS:
            first[unit].wait_recv()
        third[unit].wait_recv()
        across[unit] = send(buf.at[pl.ds(core * 16, 8)], buf.at[pl.ds(8, 8)],
                            (sp, rp), unit, partner)

    def compute(h):
        for unit in (2 * h, 2 * h + 1):
            across[unit].wait_recv()
        for copy in q_copies[h]:
            copy.wait_recv()
        own[UNITS + 2 * h].wait()
        own[UNITS + 2 * h + 1].wait()
        head_grads(h, z_hi, tiles_ref, kinds_ref, kv[h], qh, gh, slots, dq)

        def tile(t, carry):
            for i in (0, 1):
                terms = [slots[i, b, where[b * TILES + t]] for b in range(4)]
                dkv[2 * h + i, t] = ((terms[0] + terms[1]) + (terms[2] + terms[3])).astype(
                    jnp.bfloat16
                )
            return carry

        lax.fori_loop(0, TILES, tile, 0)
        for unit in (2 * h, 2 * h + 1):
            across_out[unit] = send(dkv.at[unit, pl.ds(8, 8)], part.at[unit], (tp, up), unit,
                                    partner)
        there = oq_ref.at[:, columns(x * 1024 + h * 256, 256)]
        for d in (1, 2, 3):
            out_q.append(
                send(dq.at[lax.rem(x + d, 4), :, pl.ds(h * 256, 256)], there, (os_, or_),
                     h * 3 + d - 1, along_x[d - 1])
            )
        mine = pltpu.make_async_copy(dq.at[x, :, pl.ds(h * 256, 256)], there,
                                     local_out.at[UNITS + h])
        mine.start()
        own_out.append(mine)

    def fold(unit):
        across_out[unit].wait_recv()
        summed[unit, pl.ds(core * 8, 8)] = add(dkv[unit, pl.ds(core * 16, 8)], part[unit])
        summed[unit, pl.ds(8 - core * 8, 8)] = dkv[unit, pl.ds(16 - core * 16, 8)]
        if unit in OUT_PLUS:
            near_c[unit] = send(summed.at[unit, quad(1, from_far)], near.at[unit],
                                (t1, u1), unit, left)
        else:
            near_c[unit] = send(summed.at[unit, quad(0, opposite)], near.at[unit],
                                (t1, u1), unit, right)

    def give_back(unit):
        back_c[unit] = send(summed.at[unit, quad(1, from_left)], back.at[unit],
                            (t3, u3), unit, left)

    def pass_on(unit):
        near_c[unit].wait_recv()
        if unit in OUT_PLUS:
            relay[unit] = add(near[unit], summed[unit, quad(0, opposite)])
            far_c[unit] = send(relay.at[unit], mid.at[unit], (t2, u2), unit, far_right)
        else:
            relay[unit] = add(near[unit], summed[unit, quad(1, from_far)])
            far_c[unit] = send(relay.at[unit], mid.at[unit], (t2, u2), unit, far_left)

    def turn(unit):
        far_c[unit].wait_recv()
        total[unit] = add(mid[unit], summed[unit, quad(1, from_left)])
        back_c[unit] = send(total.at[unit], back.at[unit], (t3, u3), unit, left)

    def finish(unit):
        back_c[unit].wait_recv()
        if unit in OUT_PLUS:
            back_c[unit].wait_send()
            total[unit] = add(summed[unit, quad(0, z_hi)], back[unit])
        else:
            far_c[unit].wait_recv()
            total[unit] = add(summed[unit, quad(0, z_hi)], mid[unit], back[unit])
        ref = ov_ref if unit % 2 else ok_ref
        there = ref.at[:, columns((x * HEADS + unit // 2) * HEAD, HEAD)]
        for d in (1, 2, 3):
            out_x.append(
                send(total.at[unit, lax.rem(x + d, 4)], there, (ys, yr), unit * 3 + d - 1,
                     along_x[d - 1])
            )
        mine = pltpu.make_async_copy(total.at[unit, x], there, local_out.at[unit])
        mine.start()
        own_out.append(mine)

    def find_slots(_):
        def one(t, carry):
            for b in range(4):
                found = MAXT
                for m in reversed(range(MAXT)):
                    found = jnp.where(tiles_ref[z_hi * 4 + b, m] == t, m, found)
                where[b * TILES + t] = found
            return carry

        lax.fori_loop(0, TILES, one, 0)
        for i in (0, 1):
            for b in range(4):
                slots[i, b, MAXT] = jnp.zeros((BLOCK, HEAD), jnp.float32)

    arrived = set()
    steps = {"X": spread, "Q": spread_q, "a": begin, "b": to_right, "c": hop, "d": share,
             "e": last_hop, "K": compute, "f": fold, "g": give_back, "p": pass_on, "t": turn,
             "y": finish, "w": find_slots,
             "i": lambda u: block_on(u, 0), "j": lambda u: block_on(u, 1),
             "k": lambda u: block_on(u, 3), "l": lambda u: block_on(u, 2)}
    for name in ORDER:
        steps[name[0]](int(name[1]))

    for copy in out_q + out_x:
        copy.wait_recv()
    for mine in own_out:
        mine.wait()
    sent = [c for table in (x_copies, q_copies) for copies in table.values() for c in copies]
    for table in (first, second, third, across, near_c, far_c, across_out):
        sent += list(table.values())
    sent += [back_c[unit] for unit in range(UNITS) if unit not in OUT_PLUS] + out_q + out_x
    for copy in sent:
        copy.wait_send()


ORDER = (
    "X0", "i0", "i1", "X1", "j0", "k0", "X2", "j1", "k1", "l0", "X3", "l1",
    "w0", "b2", "a2", "Q0", "b3", "a3", "c1", "Q1", "a4", "c0", "a6", "Q2",
    "a5", "c2", "b5", "Q3", "e1", "c4", "c6", "c3", "d0", "a7", "d1", "K0",
    "c5", "d2", "f0", "d3", "f1", "e4", "K1", "g0", "b7", "e6", "f2", "p0",
    "g2", "f3", "g3", "d5", "c7", "p1", "d4", "K2", "d6", "p2", "f4", "f5",
    "d7", "g5", "K3", "y0", "p3", "f6", "f7", "g7", "p4", "p6", "y2", "p5",
    "t1", "y3", "p7", "t4", "t6", "y1", "y5", "y4", "y6", "y7",
)


def copy_kernel(*refs):
    ins, outs, bufs, into, out_of = refs[:3], refs[3:6], refs[6:9], refs[9], refs[10]
    pieces = []
    for i in range(3):
        for part in range(4):
            rows = pl.ds(part * 32, 32)
            n = i * 4 + part
            pieces.append((
                pltpu.make_async_copy(ins[i].at[rows], bufs[i].at[rows], into.at[n]),
                pltpu.make_async_copy(bufs[i].at[rows], outs[i].at[rows], out_of.at[n]),
            ))
    for load, _ in pieces:
        load.start()
    for load, store in pieces:
        load.wait()
        store.start()
    for _, store in pieces:
        store.wait()


def copy_out(*arrays):
    anywhere = pl.BlockSpec(memory_space=pl.ANY)
    return pl.pallas_call(
        copy_kernel,
        name="copy_out",
        out_shape=tuple(jax.ShapeDtypeStruct(a.shape, a.dtype) for a in arrays),
        in_specs=[anywhere] * 3,
        out_specs=(anywhere,) * 3,
        scratch_shapes=[pltpu.VMEM(a.shape, a.dtype) for a in arrays]
        + [pltpu.SemaphoreType.DMA((12,))] * 2,
        compiler_params=pltpu.CompilerParams(vmem_limit_bytes=60 << 20),
    )(*arrays)


def body(queries, keys, values, output_gradient, tiles, kinds):
    smem = pl.BlockSpec(memory_space=pltpu.SMEM)
    anywhere = pl.BlockSpec(memory_space=pl.ANY)
    dma = pltpu.SemaphoreType.DMA
    bf16 = jnp.bfloat16
    unit = pltpu.VMEM((UNITS, 4, BLOCK, HEAD), bf16)
    rows = pltpu.VMEM((4, BLOCK, 1024), bf16)
    return copy_out(*pl.pallas_call(
        kernel,
        name="attention_grads",
        out_shape=(
            jax.ShapeDtypeStruct((BLOCK, 4096), bf16),
            jax.ShapeDtypeStruct((BLOCK, 2048), bf16),
            jax.ShapeDtypeStruct((BLOCK, 2048), bf16),
        ),
        in_specs=[smem, smem] + [anywhere] * 4,
        out_specs=(anywhere,) * 3,
        scratch_shapes=[pltpu.VMEM((2, TILES, BLOCK, HEAD), bf16)] * HEADS
        + [rows] * 3
        + [
            pltpu.VMEM((2, 4, MAXT + 1, BLOCK, HEAD), jnp.float32),
            pltpu.SMEM((4 * TILES,), jnp.int32),
            pltpu.VMEM((UNITS, TILES, BLOCK, HEAD), bf16),
            pltpu.VMEM((UNITS, 8, BLOCK, HEAD), bf16),
            unit,
            unit,
            unit,
            pltpu.VMEM((UNITS, 16, BLOCK, HEAD), bf16),
            unit,
            unit,
        ]
        + [dma((24,))] * 4
        + [dma((UNITS,))] * 8
        + [dma((12,))] * 2
        + [dma((24,))] * 2
        + [dma((UNITS,))] * 8
        + [dma((4 * len(EARLY),))] * 4
        + [dma((2 * UNITS,)), dma((UNITS + HEADS,))],
        compiler_params=pltpu.CompilerParams(
            collective_id=1, has_side_effects=True, vmem_limit_bytes=60 << 20
        ),
    )(tiles, kinds, queries, keys, values, output_gradient))


def solution(mesh):
    rows = P(("tm", "space"), None)
    return jax.shard_map(
        body,
        mesh=mesh,
        in_specs=(rows, rows, rows, rows, P("tm", None), P("tm", None)),
        out_specs=(rows, rows, rows),
        check_vma=False,
    )
```

```python
import functools

import jax
import jax.numpy as jnp
from jax import lax
from jax.experimental import pallas as pl
from jax.experimental.pallas import tpu as pltpu
from jax.sharding import PartitionSpec as P

HEAD = 128
BLOCK = 128
MAXT = 6
HEADS = 4
UNITS = 2 * HEADS
TILES = 24
PLUS = (1, 4, 6)
OUT_PLUS = (1, 4, 6)
EARLY = (0, 1)
MESH = pl.DeviceIdType.MESH
LOG2E = 1.4426950408889634


def place():
    tm = lax.axis_index("tm")
    space = lax.axis_index("space")
    core = lax.rem(tm, 2)
    z_lo = lax.rem(lax.div(tm, 2), 4)
    x = lax.rem(space, 4)
    z_hi = lax.div(space, 4)
    return tm, core, x, z_hi, z_hi * 4 + z_lo


def ring_peers():
    tm, core, x, z_hi, z = place()

    def at(tm_step, z_step):
        there = lax.rem(z + z_step, 8)
        return {"tm": lax.rem(tm + tm_step, 32), "space": lax.div(there, 4) * 4 + x}

    right, left, far_right, far_left = at(2, 1), at(30, 7), at(2, 5), at(30, 3)
    partner = {"tm": tm + 1 - 2 * core, "space": z_hi * 4 + x}
    along_x = [{"tm": tm, "space": z_hi * 4 + lax.rem(x + d, 4)} for d in (1, 2, 3)]
    return right, left, far_right, far_left, partner, along_x


def meet(peers):
    barrier = pltpu.get_barrier_semaphore()
    for peer in peers:
        pl.semaphore_signal(barrier, inc=1, device_id=peer, device_id_type=MESH)
    pl.semaphore_wait(barrier, len(peers))


def send(src, dst, sems, index, device):
    send_sem, recv_sem = sems
    copy = pltpu.make_async_remote_copy(
        src_ref=src,
        dst_ref=dst,
        send_sem=send_sem.at[index],
        recv_sem=recv_sem.at[index],
        device_id=device,
        device_id_type=MESH,
    )
    copy.start()
    return copy


class Pieces:
    def __init__(self):
        self.copies = []

    def wait_recv(self):
        for copy in self.copies:
            copy.wait_recv()

    def wait_send(self):
        for copy in self.copies:
            copy.wait_send()


def columns(start, width):
    return pl.ds(pl.multiple_of(start, width), width)


NT = (((1,), (1,)), ((), ()))
NN = (((1,), (0,)), ((), ()))
TN = (((0,), (0,)), ((), ()))


def dot(a, b, dims):
    return lax.dot_general(a, b, dims, preferred_element_type=jnp.float32)


def add(*terms):
    out = terms[0].astype(jnp.float32)
    for term in terms[1:]:
        out = out + term.astype(jnp.float32)
    return out.astype(jnp.bfloat16)


def head_grads(h, half, tiles_ref, kinds_ref, kv_ref, q_ref, g_ref, slots, dq_ref):
    scale = 1.0 / HEAD**0.5
    row = lax.broadcasted_iota(jnp.int32, (BLOCK, 2 * BLOCK), 0)
    col = lax.broadcasted_iota(jnp.int32, (BLOCK, 2 * BLOCK), 1)
    ahead = row - jnp.where(col >= BLOCK, col - BLOCK, col)
    one, two = pl.ds(h * 256, HEAD), pl.ds(h * 256 + HEAD, HEAD)

    def block(b, carry):
        line = half * 4 + b
        names = [tiles_ref[line, m] for m in range(MAXT)]
        kinds = [kinds_ref[line, m] for m in range(MAXT)]
        k = jnp.concatenate([kv_ref[0, t] for t in names], axis=0)
        v = jnp.concatenate([kv_ref[1, t] for t in names], axis=0)
        q = jnp.concatenate([q_ref[b, :, one], q_ref[b, :, two]], axis=0)
        g = jnp.concatenate([g_ref[b, :, one], g_ref[b, :, two]], axis=0)
        scores = dot(k, q, NT)
        masked = []
        for m in range(MAXT):
            limit = jnp.where(kinds[m] == 0, BLOCK, jnp.where(kinds[m] == 1, 0, -2 * BLOCK))
            masked.append(
                jnp.where(ahead <= limit, scores[m * BLOCK : (m + 1) * BLOCK], -jnp.inf)
            )
        scores = jnp.concatenate(masked, axis=0)
        top = jnp.max(scores, axis=0, keepdims=True)
        weights = jnp.exp2((scores - top) * (scale * LOG2E))
        probs = weights * (1.0 / jnp.sum(weights, axis=0, keepdims=True))
        low = probs.astype(jnp.bfloat16)
        grad_probs = dot(v, g, NT)
        delta = jnp.sum(low.astype(jnp.float32) * grad_probs, axis=0, keepdims=True)
        grad_scores = (probs * (grad_probs - delta) * scale).astype(jnp.bfloat16)
        slots[1, b, :MAXT] = dot(low, g, NN).reshape(MAXT, BLOCK, HEAD)
        slots[0, b, :MAXT] = dot(grad_scores, q, NN).reshape(MAXT, BLOCK, HEAD)
        grad_q = dot(grad_scores, k, TN).astype(jnp.bfloat16)
        dq_ref[b, :, one] = grad_q[:BLOCK]
        dq_ref[b, :, two] = grad_q[BLOCK:]
        return carry

    lax.fori_loop(0, 4, block, 0)


def kernel(
    tiles_ref, kinds_ref, q_in, k_in, v_in, g_in, oq_ref, ok_ref, ov_ref,
    kv0, kv1, kv2, kv3, qh, gh, dq, slots, where, dkv,
    part, near, mid, back, summed, relay, total,
    xs, xr, qs, qr, s1, r1, s2, r2, s3, r3, sp, rp,
    os_, or_, ys, yr, t1, u1, t2, u2, t3, u3, tp, up, e1s, e1r, e2s, e2r, local, local_out,
):
    tm, core, x, z_hi, z = place()
    right, left, far_right, far_left, partner, along_x = ring_peers()
    from_left = lax.div(lax.rem(z + 7, 8), 4)
    from_far = 1 - from_left
    opposite = 1 - z_hi
    kv = (kv0, kv1, kv2, kv3)
    meet([right, left, far_right, far_left, partner] + along_x)

    def quad(window, half):
        return pl.ds(window * 8 + half * 4, 4)

    def buffer(unit):
        return kv[unit // 2].at[unit % 2]

    def source(unit, to_x):
        ref = v_in if unit % 2 else k_in
        return ref.at[:, columns((to_x * HEADS + unit // 2) * HEAD, HEAD)]

    x_copies, own, q_copies = {}, {}, {}
    first, second, third, across = {}, {}, {}, {}
    out_q, out_x, own_out = [], [], []
    near_c, far_c, back_c, across_out = {}, {}, {}, {}

    def spread(h):
        for unit in (2 * h, 2 * h + 1):
            there = buffer(unit).at[z_hi * 4 + x]
            x_copies[unit] = [
                send(source(unit, lax.rem(x + d, 4)), there, (xs, xr), unit * 3 + d - 1,
                     along_x[d - 1])
                for d in (1, 2, 3)
            ]
            own[unit] = pltpu.make_async_copy(source(unit, x), there, local.at[unit])
            own[unit].start()

    def spread_q(h):
        q_copies[h] = []
        for i, (ref, to) in enumerate(((q_in, qh), (g_in, gh))):
            there = to.at[x, :, pl.ds(h * 256, 256)]
            for d in (1, 2, 3):
                q_copies[h].append(
                    send(ref.at[:, columns(lax.rem(x + d, 4) * 1024 + h * 256, 256)], there,
                         (qs, qr), h * 6 + i * 3 + d - 1, along_x[d - 1])
                )
            mine = pltpu.make_async_copy(
                ref.at[:, columns(x * 1024 + h * 256, 256)], there,
                local.at[UNITS + 2 * h + i])
            mine.start()
            own[UNITS + 2 * h + i] = mine

    def arrive(unit):
        if unit not in arrived:
            own[unit].wait()
            for copy in x_copies[unit]:
                copy.wait_recv()
            arrived.add(unit)

    def begin(unit):
        arrive(unit)
        if unit in PLUS:
            to_right(unit)
        else:
            second[unit] = send(buffer(unit).at[quad(0, z_hi)], buffer(unit).at[quad(2, z_hi)],
                                (s2, r2), unit, far_right)

    def to_right(unit):
        arrive(unit)
        first[unit] = send(buffer(unit).at[quad(0, z_hi)], buffer(unit).at[quad(2, z_hi)],
                           (s1, r1), unit, right)

    for unit in EARLY:
        first[unit] = Pieces()
        if unit not in PLUS:
            second[unit] = Pieces()

    def block_on(unit, step):
        at = z_hi * 4 + lax.rem(x + 4 - step, 4)
        if step:
            x_copies[unit][step - 1].wait_recv()
            piece = buffer(unit).at[at]
        else:
            piece = source(unit, x)
        there = buffer(unit).at[16 + at]
        if unit not in PLUS:
            second[unit].copies.append(
                send(piece, there, (e2s, e2r), unit * 4 + step, far_right))
        first[unit].copies.append(send(piece, there, (e1s, e1r), unit * 4 + step, right))
        if step == 2:
            own[unit].wait()

    def hop(unit):
        buf = buffer(unit)
        if unit in PLUS:
            first[unit].wait_recv()
            second[unit] = send(buf.at[quad(2, from_left)], buf.at[quad(0, from_left)],
                                (s2, r2), unit, far_left)
        else:
            second[unit].wait_recv()
            third[unit] = send(buf.at[quad(2, from_far)], buf.at[quad(0, from_far)],
                               (s3, r3), unit, left)

    def last_hop(unit):
        buf = buffer(unit)
        second[unit].wait_recv()
        third[unit] = send(buf.at[quad(0, opposite)], buf.at[quad(2, opposite)],
                           (s3, r3), unit, right)

    def share(unit):
        buf = buffer(unit)
        if unit not in PLUS:
            first[unit].wait_recv()
        third[unit].wait_recv()
        across[unit] = send(buf.at[pl.ds(core * 16, 8)], buf.at[pl.ds(8, 8)],
                            (sp, rp), unit, partner)

    def compute(h):
        for unit in (2 * h, 2 * h + 1):
            across[unit].wait_recv()
        for copy in q_copies[h]:
            copy.wait_recv()
        own[UNITS + 2 * h].wait()
        own[UNITS + 2 * h + 1].wait()
        head_grads(h, z_hi, tiles_ref, kinds_ref, kv[h], qh, gh, slots, dq)

        def tile(t, carry):
            for i in (0, 1):
                terms = [slots[i, b, where[b * TILES + t]] for b in range(4)]
                dkv[2 * h + i, t] = ((terms[0] + terms[1]) + (terms[2] + terms[3])).astype(
                    jnp.bfloat16
                )
            return carry

        lax.fori_loop(0, TILES, tile, 0)
        for unit in (2 * h, 2 * h + 1):
            across_out[unit] = send(dkv.at[unit, pl.ds(8, 8)], part.at[unit], (tp, up), unit,
                                    partner)
        there = oq_ref.at[:, columns(x * 1024 + h * 256, 256)]
        for d in (1, 2, 3):
            out_q.append(
                send(dq.at[lax.rem(x + d, 4), :, pl.ds(h * 256, 256)], there, (os_, or_),
                     h * 3 + d - 1, along_x[d - 1])
            )
        mine = pltpu.make_async_copy(dq.at[x, :, pl.ds(h * 256, 256)], there,
                                     local_out.at[UNITS + h])
        mine.start()
        own_out.append(mine)

    def fold(unit):
        across_out[unit].wait_recv()
        summed[unit, pl.ds(core * 8, 8)] = add(dkv[unit, pl.ds(core * 16, 8)], part[unit])
        summed[unit, pl.ds(8 - core * 8, 8)] = dkv[unit, pl.ds(16 - core * 16, 8)]
        if unit in OUT_PLUS:
            near_c[unit] = send(summed.at[unit, quad(1, from_far)], near.at[unit],
                                (t1, u1), unit, left)
        else:
            near_c[unit] = send(summed.at[unit, quad(0, opposite)], near.at[unit],
                                (t1, u1), unit, right)

    def give_back(unit):
        back_c[unit] = send(summed.at[unit, quad(1, from_left)], back.at[unit],
                            (t3, u3), unit, left)

    def pass_on(unit):
        near_c[unit].wait_recv()
        if unit in OUT_PLUS:
            relay[unit] = add(near[unit], summed[unit, quad(0, opposite)])
            far_c[unit] = send(relay.at[unit], mid.at[unit], (t2, u2), unit, far_right)
        else:
            relay[unit] = add(near[unit], summed[unit, quad(1, from_far)])
            far_c[unit] = send(relay.at[unit], mid.at[unit], (t2, u2), unit, far_left)

    def turn(unit):
        far_c[unit].wait_recv()
        total[unit] = add(mid[unit], summed[unit, quad(1, from_left)])
        back_c[unit] = send(total.at[unit], back.at[unit], (t3, u3), unit, left)

    def finish(unit):
        back_c[unit].wait_recv()
        if unit in OUT_PLUS:
            back_c[unit].wait_send()
            total[unit] = add(summed[unit, quad(0, z_hi)], back[unit])
        else:
            far_c[unit].wait_recv()
            total[unit] = add(summed[unit, quad(0, z_hi)], mid[unit], back[unit])
        ref = ov_ref if unit % 2 else ok_ref
        there = ref.at[:, columns((x * HEADS + unit // 2) * HEAD, HEAD)]
        for d in (2, 1, 3):
            out_x.append(
                send(total.at[unit, lax.rem(x + d, 4)], there, (ys, yr), unit * 3 + d - 1,
                     along_x[d - 1])
            )
        mine = pltpu.make_async_copy(total.at[unit, x], there, local_out.at[unit])
        mine.start()
        own_out.append(mine)

    def find_slots(_):
        def one(t, carry):
            for b in range(4):
                found = MAXT
                for m in reversed(range(MAXT)):
                    found = jnp.where(tiles_ref[z_hi * 4 + b, m] == t, m, found)
                where[b * TILES + t] = found
            return carry

        lax.fori_loop(0, TILES, one, 0)
        for i in (0, 1):
            for b in range(4):
                slots[i, b, MAXT] = jnp.zeros((BLOCK, HEAD), jnp.float32)

    arrived = set()
    steps = {"X": spread, "Q": spread_q, "a": begin, "b": to_right, "c": hop, "d": share,
             "e": last_hop, "K": compute, "f": fold, "g": give_back, "p": pass_on, "t": turn,
             "y": finish, "w": find_slots,
             "i": lambda u: block_on(u, 0), "j": lambda u: block_on(u, 1),
             "k": lambda u: block_on(u, 3), "l": lambda u: block_on(u, 2)}
    for name in ORDER:
        steps[name[0]](int(name[1]))

    for copy in out_q + out_x:
        copy.wait_recv()
    for mine in own_out:
        mine.wait()
    sent = [c for table in (x_copies, q_copies) for copies in table.values() for c in copies]
    for table in (first, second, third, across, near_c, far_c, across_out):
        sent += list(table.values())
    sent += [back_c[unit] for unit in range(UNITS) if unit not in OUT_PLUS] + out_q + out_x
    for copy in sent:
        copy.wait_send()


ORDER = (
    "X0", "i0", "i1", "X1", "j0", "k0", "X2", "j1", "k1", "l0", "X3", "l1",
    "w0", "b2", "a2", "Q0", "b3", "a3", "c1", "Q1", "a4", "c0", "a6", "Q2",
    "a5", "c2", "b5", "Q3", "e1", "c4", "c6", "c3", "d0", "a7", "d1", "K0",
    "c5", "d2", "f0", "d3", "f1", "e4", "K1", "g0", "b7", "e6", "f2", "p0",
    "g2", "f3", "g3", "d5", "c7", "p1", "d4", "K2", "d6", "p2", "f4", "f5",
    "d7", "g5", "K3", "y0", "p3", "f6", "f7", "g7", "p4", "p6", "y2", "p5",
    "t1", "y3", "p7", "t4", "t6", "y1", "y5", "y4", "y6", "y7",
)


def copy_kernel(*refs):
    ins, outs, bufs, into, out_of = refs[:3], refs[3:6], refs[6:9], refs[9], refs[10]
    pieces = []
    for i in range(3):
        for part in range(4):
            rows = pl.ds(part * 32, 32)
            n = i * 4 + part
            pieces.append((
                pltpu.make_async_copy(ins[i].at[rows], bufs[i].at[rows], into.at[n]),
                pltpu.make_async_copy(bufs[i].at[rows], outs[i].at[rows], out_of.at[n]),
            ))
    for load, _ in pieces:
        load.start()
    for load, store in pieces:
        load.wait()
        store.start()
    for _, store in pieces:
        store.wait()


def copy_out(*arrays):
    anywhere = pl.BlockSpec(memory_space=pl.ANY)
    return pl.pallas_call(
        copy_kernel,
        name="copy_out",
        out_shape=tuple(jax.ShapeDtypeStruct(a.shape, a.dtype) for a in arrays),
        in_specs=[anywhere] * 3,
        out_specs=(anywhere,) * 3,
        scratch_shapes=[pltpu.VMEM(a.shape, a.dtype) for a in arrays]
        + [pltpu.SemaphoreType.DMA((12,))] * 2,
        compiler_params=pltpu.CompilerParams(vmem_limit_bytes=60 << 20),
    )(*arrays)


def body(queries, keys, values, output_gradient, tiles, kinds):
    smem = pl.BlockSpec(memory_space=pltpu.SMEM)
    anywhere = pl.BlockSpec(memory_space=pl.ANY)
    dma = pltpu.SemaphoreType.DMA
    bf16 = jnp.bfloat16
    unit = pltpu.VMEM((UNITS, 4, BLOCK, HEAD), bf16)
    rows = pltpu.VMEM((4, BLOCK, 1024), bf16)
    return copy_out(*pl.pallas_call(
        kernel,
        name="attention_grads",
        out_shape=(
            jax.ShapeDtypeStruct((BLOCK, 4096), bf16),
            jax.ShapeDtypeStruct((BLOCK, 2048), bf16),
            jax.ShapeDtypeStruct((BLOCK, 2048), bf16),
        ),
        in_specs=[smem, smem] + [anywhere] * 4,
        out_specs=(anywhere,) * 3,
        scratch_shapes=[pltpu.VMEM((2, TILES, BLOCK, HEAD), bf16)] * HEADS
        + [rows] * 3
        + [
            pltpu.VMEM((2, 4, MAXT + 1, BLOCK, HEAD), jnp.float32),
            pltpu.SMEM((4 * TILES,), jnp.int32),
            pltpu.VMEM((UNITS, TILES, BLOCK, HEAD), bf16),
            pltpu.VMEM((UNITS, 8, BLOCK, HEAD), bf16),
            unit,
            unit,
            unit,
            pltpu.VMEM((UNITS, 16, BLOCK, HEAD), bf16),
            unit,
            unit,
        ]
        + [dma((24,))] * 4
        + [dma((UNITS,))] * 8
        + [dma((12,))] * 2
        + [dma((24,))] * 2
        + [dma((UNITS,))] * 8
        + [dma((4 * len(EARLY),))] * 4
        + [dma((2 * UNITS,)), dma((UNITS + HEADS,))],
        compiler_params=pltpu.CompilerParams(
            collective_id=1, has_side_effects=True, vmem_limit_bytes=60 << 20
        ),
    )(tiles, kinds, queries, keys, values, output_gradient))


def solution(mesh):
    rows = P(("tm", "space"), None)
    return jax.shard_map(
        body,
        mesh=mesh,
        in_specs=(rows, rows, rows, rows, P("tm", None), P("tm", None)),
        out_specs=(rows, rows, rows),
        check_vma=False,
    )
```
